32 devices in a mesh: section: 2 (over core), row: 4 (over z), col: 4 (over y, x).
Axes of the slice: x: 2, y: 2, z: 4, core: 2. Of those that a mesh axis runs over, the one named last changes fastest.
Arguments:
- layer_input: bfloat16 [2, 4, 512, 1536], P(None, 'row', None, 'col'), may hold values from -36 to 36
- g_out: float32 [2, 4, 512, 1536], P(None, 'row', None, 'col'), may hold values from -6 to 6
- attn_gain: float32 [2, 1536], P('section', 'col'), may hold values from 0.25 to 1.75
- w_query: bfloat16 [2, 1536, 1536], P('section', 'row', 'col'), may hold values from -0.15625 to 0.15625
- w_keyval: bfloat16 [2, 1536, 512], P('section', 'row', 'col'), may hold values from -0.15625 to 0.15625
- w_out: bfloat16 [2, 1536, 1536], P('section', 'col', 'row'), may hold values from -0.875 to 0.875
- ffn_gain: float32 [2, 1536], P('section', 'col'), may hold values from 0.25 to 1.75
- w_gate: bfloat16 [2, 1536, 8960], P('section', 'row', 'col'), may hold values from -0.15625 to 0.15625
- w_up: bfloat16 [2, 1536, 8960], P('section', 'row', 'col'), may hold values from -0.15625 to 0.15625
- w_down: bfloat16 [2, 8960, 1536], P('section', 'col', 'row'), may hold values from -0.0625 to 0.0625
Outputs:
- acts: bfloat16 [2, 2, 4, 512, 1536], P('section', None, 'row', None, 'col')
- grads_in: bfloat16 [2, 2, 4, 512, 1536], P('section', None, 'row', None, 'col')
- d_attn_gain: float32 [2, 1536], P('section', 'col')
- d_query: float32 [2, 1536, 1536], P('section', 'row', 'col')
- d_keyval: float32 [2, 1536, 512], P('section', 'row', 'col')
- d_out: float32 [2, 1536, 1536], P('section', 'col', 'row')
- d_ffn_gain: float32 [2, 1536], P('section', 'col')
- d_gate: float32 [2, 1536, 8960], P('section', 'row', 'col')
- d_up: float32 [2, 1536, 8960], P('section', 'row', 'col')
- d_down: float32 [2, 8960, 1536], P('section', 'col', 'row')
The draws below stay inside these ranges and needn't reach their ends.
All inputs are finite; a program needn't handle non-finite values.
Results may differ from the reference program's by a relative error of at most 0.028.
Values may be sent and summed in bfloat16 or wider, within the bound.
No kernel may reach another device: no remote copies, remote signals or barrier semaphores. Data moves between devices by JAX's collectives and lax.ppermute only.
A program may use at most 320 MiB of HBM per device.

```python
import math
import jax
import jax.numpy as jnp
from jax import lax

D = 1536
H = 12
KVH = 2
HD = 128
FF = 8960
SPAN = 4
MB = 2
SEGL = 512
SEQ = 2048
PIECES = 4


def draw_layer_input(key, part):
    base_key, row_key, col_key = jax.random.split(key, 3)
    shape = (MB, PIECES, SEGL, D)
    col_scale = jnp.exp(jax.random.uniform(col_key, (D,), jnp.float32, math.log(0.3), math.log(3.0)))
    row_scale = jnp.exp(jax.random.uniform(row_key, (MB, PIECES, SEGL, 1), jnp.float32, math.log(0.3), math.log(3.0)))
    base = jnp.clip(jax.random.normal(base_key, shape, jnp.float32), -4.0, 4.0)
    return (base * row_scale * col_scale).astype(jnp.bfloat16)


def level_of(stream_key, shape, cuts, low, high):
    factor_of, own = 1.0, jax.random.fold_in(stream_key, 6)
    for position, parts in cuts:
        steps = jnp.exp(jax.random.uniform(jax.random.fold_in(own, position), (parts,), jnp.float32, low / len(cuts), high / len(cuts)))
        factor_of = factor_of * jnp.repeat(steps, shape[position] // parts).reshape([-1 if axis == position else 1 for axis in range(len(shape))])
    return factor_of


def bell_draw(own_key, extent, spread, reach, cuts=(), held_as=jnp.bfloat16):
    loudness = level_of(own_key, extent, cuts, -0.22, 0.18) if cuts else 1.0
    entries = jax.random.normal(own_key, extent, jnp.float32) * spread * loudness
    return jnp.minimum(jnp.maximum(entries, -reach), reach).astype(held_as)


def setup_inputs(seed: int = 0) -> dict:
    key_of = jax.random.split(jax.random.key(seed), 11)
    return {
        "layer_input": draw_layer_input(jax.random.fold_in(key_of[10], 71), 0),
        "g_out": bell_draw(key_of[1], (MB, PIECES, SEGL, D), 1.0, 6.0, ((1, 4), (3, 4)), jnp.float32),
        "attn_gain": jnp.clip(1.0 + 0.15 * jax.random.normal(key_of[2], (2, D), jnp.float32), 0.25, 1.75),
        "w_query": bell_draw(key_of[3], (2, D, H * HD), D ** -0.5, 0.15625, ((0, 2), (1, 4), (2, 4))),
        "w_keyval": bell_draw(key_of[4], (2, D, 2 * KVH * HD), D ** -0.5, 0.15625, ((0, 2), (1, 4), (2, 4))),
        "w_out": bell_draw(key_of[5], (2, H * HD, D), (H * HD // 32) ** -0.5, 0.875, ((0, 2), (1, 4), (2, 4))),
        "ffn_gain": jnp.clip(1.0 + 0.15 * jax.random.normal(key_of[6], (2, D), jnp.float32), 0.25, 1.75),
        "w_gate": bell_draw(key_of[7], (2, D, FF), D ** -0.5, 0.15625, ((0, 2), (1, 4), (2, 4))),
        "w_up": bell_draw(key_of[8], (2, D, FF), D ** -0.5, 0.15625, ((0, 2), (1, 4), (2, 4))),
        "w_down": bell_draw(key_of[9], (2, FF, D), FF ** -0.5, 0.0625, ((0, 2), (1, 4), (2, 4))),
    }


EPS = 1e-06
THETA = 1000000.0

@jax.custom_vjp
def low(v):
    return lax.optimization_barrier(v.astype(jnp.bfloat16)).astype(jnp.float32)

@jax.custom_vjp
def low_back(v):
    return v

def low_keep(v):
    return (low(v), None)

def low_pass(kept, grad):
    return (grad,)

def back_keep(v):
    return (v, None)

def back_low(kept, grad):
    return (low(grad),)
low.defvjp(low_keep, low_pass)
low_back.defvjp(back_keep, back_low)

def rotate_half(values):
    half = values.shape[-1] // 2
    return jnp.concatenate([-values[..., half:], values[..., :half]], axis=-1)

def rope_tables(positions, head_size):
    half = head_size // 2
    freqs = THETA ** (-(jnp.arange(half, dtype=jnp.float32) * 2.0) / head_size)
    angles = positions.astype(jnp.float32)[:, None] * freqs[None, :]
    angles = jnp.concatenate([angles, angles], axis=-1)
    return (jnp.cos(angles), jnp.sin(angles))

def rotate(values, cosine, sine):
    return values * cosine + rotate_half(values) * sine

def matmul(left, right):
    return jnp.matmul(left, right, precision=lax.Precision.HIGHEST)

def normalize(resid, gain):
    inverse = lax.rsqrt(lax.optimization_barrier(jnp.mean(resid * resid, axis=-1, keepdims=True)) + EPS)
    return low(resid * inverse * gain)

def attend(pieces):
    queries, keys, values = pieces
    group = H // KVH
    keys = jnp.repeat(keys, group, axis=1)
    values = jnp.repeat(values, group, axis=1)
    length = queries.shape[0]
    scale = 1.0 / math.sqrt(HD)
    scores = low_back(jnp.einsum('qhd,khd->hqk', queries, keys, precision=lax.Precision.HIGHEST) * scale)
    index = jnp.arange(length, dtype=jnp.int32)
    allowed = index[None, :] <= index[:, None]
    unnormed = jnp.where(allowed[None], jnp.exp(scores), 0.0)
    probs = unnormed / lax.optimization_barrier(jnp.sum(unnormed, axis=-1, keepdims=True))
    return jnp.einsum('hqk,khd->qhd', low(probs), values, precision=lax.Precision.HIGHEST)

def layer(resid, params, cosine, sine):
    attn_gain, w_query, w_keyval, w_out, ffn_gain, w_gate, w_up, w_down = params
    count, length, width = resid.shape
    normed = normalize(resid, attn_gain)
    query_raw = low_back(matmul(normed, w_query)).reshape(count, length, H, HD)
    pairs = matmul(normed, w_keyval).reshape(count, length, KVH, 2, HD)
    key_raw = low_back(pairs[:, :, :, 0, :])
    values = low(low_back(pairs[:, :, :, 1, :]))
    cos_wide = cosine[None, :, None, :]
    sin_wide = sine[None, :, None, :]
    queries = low(rotate(query_raw, cos_wide, sin_wide))
    keys = low(rotate(key_raw, cos_wide, sin_wide))
    attended = lax.map(jax.checkpoint(attend), (queries, keys, values))
    attended = low(low_back(attended.reshape(count, length, H * HD)))
    middle = resid + low_back(matmul(attended, w_out))
    normed_ffn = normalize(middle, ffn_gain)
    gate = low_back(matmul(normed_ffn, w_gate))
    up = low_back(matmul(normed_ffn, w_up))
    hidden = low(jax.nn.silu(gate) * up)
    return middle + low_back(matmul(hidden, w_down))

def to_sequences(array):
    groups = PIECES // SPAN
    return array.reshape(MB * groups, SPAN * SEGL, D)

def from_sequences(array):
    return array.reshape(MB, PIECES, SEGL, D)

def reference(layer_input, g_out, attn_gain, w_query, w_keyval, w_out, ffn_gain, w_gate, w_up, w_down):
    inputs = to_sequences(layer_input.astype(jnp.float32))
    cotangent = to_sequences(g_out.astype(jnp.float32))
    positions = jnp.arange(SEQ, dtype=jnp.int32)
    cosine, sine = rope_tables(positions, HD)
    params = tuple((p.astype(jnp.float32) for p in (attn_gain, w_query, w_keyval, w_out, ffn_gain, w_gate, w_up, w_down)))

    def forward(first_in, weights, nudge):
        first = tuple((w[0] for w in weights))
        second = tuple((w[1] for w in weights))
        middle = low_back(low(layer(first_in, first, cosine, sine)) + nudge)
        return (layer(middle, second, cosine, sine), middle)
    nudge = jnp.zeros_like(inputs)
    final, pullback, middle = jax.vjp(forward, inputs, params, nudge, has_aux=True)
    grad_input, grad_params, grad_middle = pullback(cotangent)
    acts = jnp.stack([from_sequences(middle), from_sequences(final)]).astype(jnp.bfloat16)
    grads_in = jnp.stack([from_sequences(grad_input), from_sequences(grad_middle)]).astype(jnp.bfloat16)
    return (acts, grads_in, grad_params[0], grad_params[1], grad_params[2], grad_params[3], grad_params[4], grad_params[5], grad_params[6], grad_params[7])
```

```python
import math

import jax
import jax.numpy as jnp
from jax import lax
from jax.sharding import PartitionSpec as P

HD = 128
SPAN = 4
EPS = 1e-06
THETA = 1000000.0
BF = jnp.bfloat16
F32 = jnp.float32


def dot(left, right, left_dim, right_dim):
    return lax.dot_general(
        left, right, (((left_dim,), (right_dim,)), ((), ())), preferred_element_type=F32
    )


def rotate_half(values):
    half = values.shape[-1] // 2
    return jnp.concatenate([-values[..., half:], values[..., :half]], axis=-1)


def rope_tables(positions, head_size):
    half = head_size // 2
    freqs = THETA ** (-(jnp.arange(half, dtype=F32) * 2.0) / head_size)
    angles = positions.astype(F32)[:, None] * freqs[None, :]
    angles = jnp.concatenate([angles, angles], axis=-1)
    return (jnp.cos(angles), jnp.sin(angles))


def rotate(values, cosine, sine):
    return values * cosine + rotate_half(values) * sine


def rotate_back(values, cosine, sine):
    return values * cosine - rotate_half(values * sine)


def over_col(block, step):
    count = lax.axis_size("col")
    return lax.ppermute(block, "col", [(i, i ^ step) for i in range(count)])


def over_section(block):
    return lax.ppermute(block, "section", [(0, 1), (1, 0)])


def along_row(block, steps):
    count = lax.axis_size("row")
    route = [(i, i + steps) for i in range(count) if 0 <= i % SPAN + steps < SPAN]
    return lax.ppermute(block, "row", route)


def gather_blocks(own):
    half = own.shape[0] // 2
    first = over_col(own, 1)
    second = over_col(own, 2)
    third_low = over_col(first[:half], 2)
    third_high = over_col(second[half:], 1)
    return own, first, second, jnp.concatenate([third_low, third_high], axis=0)


def gather_tokens(own):
    return jnp.concatenate(gather_blocks(own), axis=0)


def scatter_tokens(partial):
    blocks = jnp.split(partial, 4, axis=0)
    half = blocks[0].shape[0] // 2
    low = over_col(blocks[3][:half], 1)
    high = over_col(blocks[3][half:], 2)
    second_low = (blocks[2][:half].astype(F32) + low.astype(F32)).astype(BF)
    first_high = (blocks[1][half:].astype(F32) + high.astype(F32)).astype(BF)
    from_first = over_col(jnp.concatenate([blocks[1][:half], first_high], axis=0), 1)
    from_second = over_col(jnp.concatenate([second_low, blocks[2][half:]], axis=0), 2)
    return blocks[0].astype(F32) + from_first.astype(F32) + from_second.astype(F32)


def norm(resid, gain):
    inverse = lax.rsqrt(jnp.mean(resid * resid, axis=1, keepdims=True) + EPS)
    return (resid * inverse * gain[None, :]).astype(BF), inverse


def norm_backward(grad_normed, resid, inverse, gain):
    scaled = resid * inverse
    grad_gain = jnp.sum(grad_normed * scaled, axis=0)
    grad_scaled = grad_normed * gain[None, :]
    mean_term = jnp.mean(grad_scaled * scaled, axis=1, keepdims=True)
    return inverse * (grad_scaled - scaled * mean_term), grad_gain


def local(layer_input, g_out, attn_gain, w_query, w_keyval, w_out, ffn_gain, w_gate, w_up, w_down):
    section = lax.axis_index("section")
    col = lax.axis_index("col")
    peer = lax.axis_index("row") % SPAN
    cols = lax.axis_size("col")
    is_first = section == 0
    is_key = col % 2 == 0
    rows = layer_input.shape[2]
    width = layer_input.shape[3]
    own_rows = rows // cols
    full = width * cols
    heads = w_query.shape[2] // HD
    query_cols = w_query.shape[2]
    key_cols = w_keyval.shape[2]
    units = w_gate.shape[2]
    padded = -(-units // 256) * 256
    scale = 1.0 / math.sqrt(HD)

    def by_section(first, second):
        return jnp.where(is_first, first, second)

    def xor_rows(block):
        return jnp.concatenate(
            [lax.dynamic_slice_in_dim(block, (col ^ k) * own_rows, own_rows, 0) for k in range(cols)],
            axis=0,
        )

    def reorder(block, k):
        parts = jnp.split(block, cols, axis=0)
        return jnp.concatenate([parts[m ^ k] for m in range(cols)], axis=0)

    def gather_width(block):
        parts = [reorder(part, k) for k, part in enumerate(gather_blocks(xor_rows(block)))]
        total = jnp.zeros((block.shape[0], full), block.dtype)
        for k, part in enumerate(parts):
            total = lax.dynamic_update_slice_in_dim(total, part, (col ^ k) * width, 1)
        return total

    def tokens_from_width(block):
        total = jnp.zeros((own_rows, full), block.dtype)
        for k in range(cols):
            part = lax.dynamic_slice_in_dim(block, (col ^ k) * own_rows, own_rows, 0)
            if k:
                part = over_col(part, k)
            total = lax.dynamic_update_slice_in_dim(total, part, (col ^ k) * width, 1)
        return total

    def width_from_tokens(block):
        total = jnp.zeros((rows, width), block.dtype)
        for k in range(cols):
            part = lax.dynamic_slice_in_dim(block, (col ^ k) * width, width, 1)
            if k:
                part = over_col(part, k)
            total = lax.dynamic_update_slice_in_dim(total, part, (col ^ k) * own_rows, 0)
        return total

    gains_own = jnp.stack([attn_gain[0], ffn_gain[0]])
    gains_other = over_section(gains_own)
    gains_part = jnp.stack([by_section(gains_own, gains_other), by_section(gains_other, gains_own)])
    gains = jnp.zeros((2, 2, full), F32)
    for k in range(cols):
        part = over_col(gains_part, k) if k else gains_part
        gains = lax.dynamic_update_slice_in_dim(gains, part, (col ^ k) * width, 2)

    pad = ((0, 0), (0, padded - units))
    gate_own = jnp.pad(w_gate[0], pad)
    up_own = jnp.pad(w_up[0], pad)
    down_own = jnp.pad(w_down[0].T, pad)
    attn_own = jnp.concatenate([w_query[0], w_keyval[0], w_out[0].T], axis=1)
    shard = attn_own.shape[0]
    half_rows = shard // 2
    half_units = padded // 2

    def both_layers(low, high):
        got = over_section(by_section(high, low))
        return by_section(low, got), by_section(got, high)

    attn_parts = both_layers(attn_own[:half_rows], attn_own[half_rows:])
    gate_up_parts = both_layers(gate_own, up_own)
    down_parts = both_layers(down_own[:, :half_units], down_own[:, half_units:])
    weights = []
    for layer in range(2):
        attn_w = lax.all_gather(attn_parts[layer], ("row", "section"), axis=0, tiled=True)
        gate_up_w = lax.all_gather(gate_up_parts[layer], ("section", "row"), axis=0, tiled=True)
        down_w = lax.all_gather(down_parts[layer], ("section", "row"), axis=0, tiled=True)
        weights.append(
            (
                attn_w[:, :query_cols],
                attn_w[:, query_cols : query_cols + key_cols],
                attn_w[:, query_cols + key_cols :],
                gate_up_w[:full],
                gate_up_w[full:],
                down_w[:full],
                down_w[full:],
            )
        )

    order = jnp.concatenate(
        [(col ^ k) * own_rows + jnp.arange(own_rows, dtype=jnp.int32) for k in range(cols)]
    )
    positions = peer * rows + order
    cosine, sine = rope_tables(positions, HD)
    key_positions = jnp.concatenate([(peer - k) * rows + order for k in range(SPAN)])
    allowed = (key_positions[None, :] <= positions[:, None]) & (key_positions[None, :] >= 0)

    def swap_pairs(keys):
        parts = keys.reshape(SPAN, cols // 2, 2, own_rows, HD)
        return jnp.concatenate([parts[:, :, 1:], parts[:, :, :1]], axis=2).reshape(keys.shape)

    def layer_forward(resid, normed, inverse_attn, layer):
        w_q, w_kv, w_o, w_g, w_u, w_d0, w_d1 = weights[layer]
        query_raw = dot(normed, w_q, 1, 0).reshape(rows, heads, HD)
        queries = rotate(query_raw, cosine[:, None, :], sine[:, None, :]).astype(BF)
        own_cols = dot(normed, w_kv, 1, 0)
        own_cols = jnp.where(is_key, rotate(own_cols, cosine, sine), own_cols).astype(BF)
        mine = jnp.concatenate(
            [own_cols] + [along_row(own_cols, k) for k in range(1, SPAN)], axis=0
        )
        partner = swap_pairs(over_col(mine, 1))
        keys = jnp.where(is_key, mine, partner)
        values = jnp.where(is_key, partner, mine)
        scores = jnp.einsum("qhd,kd->hqk", queries, keys, preferred_element_type=F32) * scale
        unnormed = jnp.where(allowed[None], jnp.exp(scores), 0.0)
        total = jnp.sum(unnormed, axis=-1)
        probs = unnormed / total[..., None]
        attended = jnp.einsum("hqk,kd->qhd", probs.astype(BF), values, preferred_element_type=F32)
        attended = attended.reshape(rows, heads * HD).astype(BF)
        middle = resid + scatter_tokens(dot(attended, w_o, 1, 1).astype(BF))
        normed_own, inverse_ffn = norm(middle, gains[layer, 1])
        normed_ffn = gather_tokens(normed_own)
        gate = dot(normed_ffn, w_g, 1, 0)
        up = dot(normed_ffn, w_u, 1, 0)
        hidden = (jax.nn.silu(gate) * up).astype(BF)
        down = dot(hidden[:, :half_units], w_d0, 1, 1) + dot(hidden[:, half_units:], w_d1, 1, 1)
        result = middle + scatter_tokens(down.astype(BF))
        kept = (
            resid,
            inverse_attn,
            normed,
            queries,
            keys,
            values,
            jnp.log(total),
            attended,
            middle,
            inverse_ffn,
            normed_ffn,
            gate,
            up,
            hidden,
        )
        return result, kept

    def swap_add(left, keep, send):
        got = over_section(dot(left, send, 0, 0).astype(BF))
        return (dot(left, keep, 0, 0) + got.astype(F32)).astype(BF)

    def scatter_rows(total):
        return lax.psum_scatter(total, "row", scatter_dimension=0, tiled=True)

    def layer_backward(grad_own, grad_branch, kept, layer):
        w_q, w_kv, w_o, w_g, w_u, w_d0, w_d1 = weights[layer]
        (
            resid,
            inverse_attn,
            normed,
            queries,
            keys,
            values,
            log_total,
            attended,
            middle,
            inverse_ffn,
            normed_ffn,
            gate,
            up,
            hidden,
        ) = kept
        low, high = hidden[:, :half_units], hidden[:, half_units:]
        down_sum = scatter_rows(swap_add(grad_branch, by_section(low, high), by_section(high, low)))
        grad_hidden = jnp.concatenate(
            [dot(grad_branch, w_d0, 1, 0), dot(grad_branch, w_d1, 1, 0)], axis=1
        )
        sigma = jax.nn.sigmoid(gate)
        grad_gate_act = (grad_hidden * up * sigma * (1.0 + gate * (1.0 - sigma))).astype(BF)
        grad_up_act = (grad_hidden * gate * sigma).astype(BF)
        grad_normed_ffn = scatter_tokens(
            (dot(grad_gate_act, w_g, 1, 1) + dot(grad_up_act, w_u, 1, 1)).astype(BF)
        )
        gate_up_sum = scatter_rows(
            swap_add(
                normed_ffn,
                by_section(grad_gate_act, grad_up_act),
                by_section(grad_up_act, grad_gate_act),
            )
        )
        grad_middle, grad_gain_ffn = norm_backward(
            grad_normed_ffn, middle, inverse_ffn, gains[layer, 1]
        )
        grad_middle = grad_own + grad_middle
        grad_attn_out = gather_tokens(grad_middle.astype(BF))
        grad_wout = dot(grad_attn_out, attended, 0, 0)
        grad_attended = dot(grad_attn_out, w_o, 1, 0).astype(BF).reshape(rows, heads, HD)
        scores = jnp.einsum("qhd,kd->hqk", queries, keys, preferred_element_type=F32) * scale
        probs = jnp.where(allowed[None], jnp.exp(scores - log_total[..., None]), 0.0)
        grad_probs = jnp.einsum("qhd,kd->hqk", grad_attended, values, preferred_element_type=F32)
        grad_scores = (
            probs * (grad_probs - jnp.sum(probs * grad_probs, axis=-1, keepdims=True))
        ).astype(BF)
        grad_queries = (
            jnp.einsum("hqk,kd->qhd", grad_scores, keys, preferred_element_type=F32) * scale
        )
        grad_keys = (
            jnp.einsum("hqk,qhd->kd", grad_scores, queries, preferred_element_type=F32) * scale
        )
        grad_values = jnp.einsum(
            "hqk,qhd->kd", probs.astype(BF), grad_attended, preferred_element_type=F32
        )
        partner = swap_pairs(
            over_col(jnp.where(is_key, grad_values, grad_keys).astype(BF), 1)
        ).astype(F32)
        grad_cols = jnp.where(is_key, grad_keys, grad_values) + partner
        pieces = jnp.split(grad_cols, SPAN, axis=0)
        grad_mine = pieces[0]
        for k in range(1, SPAN):
            grad_mine = grad_mine + along_row(pieces[k].astype(BF), -k).astype(F32)
        grad_mine = jnp.where(is_key, rotate_back(grad_mine, cosine, sine), grad_mine).astype(BF)
        grad_query_raw = (
            rotate_back(grad_queries, cosine[:, None, :], sine[:, None, :])
            .astype(BF)
            .reshape(rows, heads * HD)
        )
        grad_normed = scatter_tokens(
            (dot(grad_query_raw, w_q, 1, 1) + dot(grad_mine, w_kv, 1, 1)).astype(BF)
        )
        attn_grads = jnp.concatenate(
            [
                dot(normed, grad_query_raw, 0, 0).astype(BF),
                dot(normed, grad_mine, 0, 0).astype(BF),
                grad_wout.astype(BF),
            ],
            axis=1,
        ).reshape(-1, 2, half_rows, attn_own.shape[1])
        got = over_section(by_section(attn_grads[:, 1], attn_grads[:, 0])).astype(F32)
        attn_grads = (by_section(attn_grads[:, 0], attn_grads[:, 1]).astype(F32) + got).astype(BF)
        attn_sum = scatter_rows(attn_grads.reshape(-1, attn_own.shape[1]))
        grad_resid, grad_gain_attn = norm_backward(
            grad_normed, resid, inverse_attn, gains[layer, 0]
        )
        return (
            grad_middle + grad_resid,
            (attn_sum, gate_up_sum, down_sum),
            jnp.stack([grad_gain_attn, grad_gain_ffn]),
        )

    x_full = gather_width(lax.dynamic_index_in_dim(layer_input[:, 0], section, 0, keepdims=False))
    top = lax.dynamic_index_in_dim(g_out[:, 0], section, 0, keepdims=False)
    normed, inverse = norm(x_full.astype(F32), gains[0, 0])
    result, kept_0 = layer_forward(x_full[:own_rows].astype(F32), normed, inverse[:own_rows], 0)
    act_0 = result.astype(BF)
    resid = act_0.astype(F32)
    normed_own, inverse = norm(resid, gains[1, 0])
    result, kept_1 = layer_forward(resid, gather_tokens(normed_own), inverse, 1)
    act_1 = result.astype(BF)

    top_branch = gather_width(top.astype(BF))
    top_own = tokens_from_width(top)
    grad_1, sums_1, gain_grads_1 = layer_backward(top_own, top_branch, kept_1, 1)
    grad_1 = grad_1.astype(BF)
    grad_0, sums_0, gain_grads_0 = layer_backward(
        grad_1.astype(F32), gather_tokens(grad_1), kept_0, 0
    )
    grad_0 = grad_0.astype(BF)

    def by_layer(first, second):
        first, second = width_from_tokens(first), width_from_tokens(second)
        got = over_section(by_section(second, first))
        return jnp.stack([by_section(first, got), by_section(got, second)])

    acts = by_layer(act_0, act_1)
    grads_in = by_layer(grad_0, grad_1)

    def to_layer(zero, one):
        one_low = lax.ppermute(one, "section", [(0, 1)])
        zero_high = lax.ppermute(zero, "section", [(1, 0)])
        return by_section(zero, one_low), by_section(zero_high, one)

    attn_final = jnp.concatenate(to_layer(sums_0[0], sums_1[0]), axis=0).astype(F32)
    final_gate, final_up = to_layer(sums_0[1], sums_1[1])
    down_final = jnp.concatenate(to_layer(sums_0[2], sums_1[2]), axis=1)[:, :units]
    gain_sums = lax.psum(jnp.stack([gain_grads_0, gain_grads_1]), ("section", "row", "col"))
    gain_sums = lax.dynamic_index_in_dim(gain_sums, section, 0, keepdims=False)
    gain_sums = lax.dynamic_slice_in_dim(gain_sums, col * width, width, 1)

    return (
        acts.reshape(1, 2, 1, rows, width),
        grads_in.reshape(1, 2, 1, rows, width),
        gain_sums[:1],
        attn_final[None, :, :query_cols],
        attn_final[None, :, query_cols : query_cols + key_cols],
        attn_final[:, query_cols + key_cols :].T[None],
        gain_sums[1:],
        final_gate[None, :, :units].astype(F32),
        final_up[None, :, :units].astype(F32),
        down_final.astype(F32).T[None],
    )


def solution(mesh):
    placed = (
        P(None, "row", None, "col"),
        P(None, "row", None, "col"),
        P("section", "col"),
        P("section", "row", "col"),
        P("section", "row", "col"),
        P("section", "col", "row"),
        P("section", "col"),
        P("section", "row", "col"),
        P("section", "row", "col"),
        P("section", "col", "row"),
    )
    return jax.shard_map(
        local,
        mesh=mesh,
        in_specs=placed,
        out_specs=(
            P("section", None, "row", None, "col"),
            P("section", None, "row", None, "col"),
            P("section", "col"),
            P("section", "row", "col"),
            P("section", "row", "col"),
            P("section", "col", "row"),
            P("section", "col"),
            P("section", "row", "col"),
            P("section", "row", "col"),
            P("section", "col", "row"),
        ),
        check_vma=False,
    )
```

```python
import functools
import math

import jax
import jax.numpy as jnp
from jax import lax
from jax.experimental import pallas as pl
from jax.experimental.pallas import tpu as pltpu
from jax.sharding import PartitionSpec as P


HD = 128
SPAN = 4
EPS = 1e-06
THETA = 1000000.0
BF = jnp.bfloat16
F32 = jnp.float32


def dot(left, right, left_dim, right_dim):
    return lax.dot_general(
        left, right, (((left_dim,), (right_dim,)), ((), ())), preferred_element_type=F32
    )


def rope_tables(positions, head_size):
    half = head_size // 2
    freqs = THETA ** (-(jnp.arange(half, dtype=F32) * 2.0) / head_size)
    angles = positions.astype(F32)[:, None] * freqs[None, :]
    angles = jnp.concatenate([angles, angles], axis=-1)
    return (jnp.cos(angles), jnp.sin(angles))


ROW = "row"


def after(value, *others):
    return lax.optimization_barrier((value, *others))


def over_col(block, step):
    count = lax.axis_size("col")
    return lax.ppermute(block, "col", [(i, i ^ step) for i in range(count)])


def over_section(block):
    return lax.ppermute(block, "section", [(0, 1), (1, 0)])


def along_row(block, steps):
    count = lax.axis_size(ROW)
    route = [(i, i + steps) for i in range(count) if 0 <= i % SPAN + steps < SPAN]
    return lax.ppermute(block, ROW, route)


def gather_blocks(own):
    half = own.shape[0] // 2
    first = over_col(own, 1)
    second = over_col(own, 2)
    third_low = over_col(first[:half], 2)
    third_high = over_col(second[half:], 1)
    return own, first, second, jnp.concatenate([third_low, third_high], axis=0)


def gather_tokens(own):
    return jnp.concatenate(gather_blocks(own), axis=0)


def scatter_tokens(partial):
    blocks = jnp.split(partial, 4, axis=0)
    got = [over_col(blocks[k], k).astype(F32) for k in (3, 1, 2)]
    return blocks[0].astype(F32) + got[0] + got[1] + got[2]


def norm(resid, gain):
    inverse = lax.rsqrt(jnp.mean(resid * resid, axis=1, keepdims=True) + EPS)
    return (resid * inverse * gain[None, :]).astype(BF), inverse


def norm_backward(grad_normed, resid, inverse, gain):
    scaled = resid * inverse
    grad_gain = jnp.sum(grad_normed * scaled, axis=0)
    grad_scaled = grad_normed * gain[None, :]
    mean_term = jnp.mean(grad_scaled * scaled, axis=1, keepdims=True)
    return inverse * (grad_scaled - scaled * mean_term), grad_gain


def qkv_kernel(heads, x_ref, w_ref, cos_ref, sign_ref, q_ref, kv_ref):
    raw = jnp.dot(x_ref[...], w_ref[...], preferred_element_type=F32)
    cosine, signed = cos_ref[...], sign_ref[...]
    for h in range(heads + 1):
        z = raw[:, h * HD : (h + 1) * HD]
        z = (z * cosine + pltpu.roll(z, HD // 2, 1) * signed).astype(BF)
        if h < heads:
            q_ref[:, h * HD : (h + 1) * HD] = z
        else:
            kv_ref[:, :HD] = z
    kv_ref[:, HD:] = raw[:, (heads + 1) * HD :].astype(BF)


def project_turn(normed, weight, cosine, signed, heads):
    rows, depth = normed.shape
    step = rows // 2
    cols = (heads + 2) * HD
    return pl.pallas_call(
        functools.partial(qkv_kernel, heads),
        grid=(2,),
        in_specs=[
            pl.BlockSpec((step, depth), lambda i: (i, 0)),
            pl.BlockSpec((depth, cols), lambda i: (0, 0)),
            pl.BlockSpec((step, HD), lambda i: (i, 0)),
            pl.BlockSpec((step, HD), lambda i: (i, 0)),
        ],
        out_specs=[
            pl.BlockSpec((step, heads * HD), lambda i: (i, 0)),
            pl.BlockSpec((step, 2 * HD), lambda i: (i, 0)),
        ],
        out_shape=[
            jax.ShapeDtypeStruct((rows, heads * HD), BF),
            jax.ShapeDtypeStruct((rows, 2 * HD), BF),
        ],
        cost_estimate=pl.CostEstimate(
            flops=2 * rows * depth * cols,
            bytes_accessed=2 * (rows * depth + depth * cols + rows * cols),
            transcendentals=0,
        ),
        name="project_turn",
    )(normed, weight, cosine, signed)


def attend_kernel(scale, peer_ref, col_ref, row_ref, q_ref, *refs):
    pieces, (o_ref, lse_ref, e_ref, total_ref, acc_ref) = refs[:SPAN], refs[SPAN:]
    peer = peer_ref[0]
    q = q_ref[...]

    def exps(k):
        s = lax.dot_general(
            pieces[k][:, :HD], q, (((1,), (1,)), ((), ())), preferred_element_type=F32
        )
        return jnp.exp(s * scale)

    e = jnp.where(col_ref[...] <= row_ref[...], exps(0), 0.0)
    e_ref[0] = e
    total_ref[...] = jnp.sum(e, axis=0, keepdims=True)
    for k in range(1, SPAN):

        @pl.when(peer >= k)
        def _():
            e = exps(k)
            e_ref[k] = e
            total_ref[...] += jnp.sum(e, axis=0, keepdims=True)

    total = total_ref[...]
    lse_ref[0] = jnp.log(total)
    shrink = jnp.where(total > 1.0, 2.0**-64, 1.0)
    inverse = 1.0 / (total * shrink)

    def term(k):
        p = ((e_ref[k] * shrink) * inverse).astype(BF)
        return lax.dot_general(
            pieces[k][:, HD:], p, (((0,), (0,)), ((), ())), preferred_element_type=F32
        )

    acc_ref[...] = term(0)
    for k in range(1, SPAN):

        @pl.when(peer >= k)
        def _():
            acc_ref[...] += term(k)

    o_ref[...] = acc_ref[...].T.astype(BF)


def attend(queries, pieces, peer, order, heads, scale):
    rows = queries.shape[0]
    full = SPAN * rows
    return pl.pallas_call(
        functools.partial(attend_kernel, scale),
        grid=(heads,),
        in_specs=[
            pl.BlockSpec(memory_space=pltpu.SMEM),
            pl.BlockSpec((rows, 1), lambda h: (0, 0)),
            pl.BlockSpec((1, rows), lambda h: (0, 0)),
            pl.BlockSpec((rows, HD), lambda h: (0, h)),
            *[pl.BlockSpec((rows, 2 * HD), lambda h: (0, 0))] * SPAN,
        ],
        out_specs=[
            pl.BlockSpec((rows, HD), lambda h: (0, h)),
            pl.BlockSpec((1, 1, rows), lambda h: (h, 0, 0)),
        ],
        out_shape=[
            jax.ShapeDtypeStruct((rows, heads * HD), BF),
            jax.ShapeDtypeStruct((heads, 1, rows), F32),
        ],
        scratch_shapes=[
            pltpu.VMEM((SPAN, rows, rows), F32),
            pltpu.VMEM((1, rows), F32),
            pltpu.VMEM((HD, rows), F32),
        ],
        cost_estimate=pl.CostEstimate(
            flops=4 * heads * rows * full * HD,
            bytes_accessed=4 * rows * HD * (heads + SPAN),
            transcendentals=heads * rows * full,
        ),
        name="attend",
    )(peer, order[:, None], order[None, :], queries, *pieces)


def attend_back_kernel(scale, peer_ref, col_ref, row_ref, cos_ref, sign_ref, q_ref, do_ref, lse_ref, *refs):
    pieces = refs[:SPAN]
    dq_ref, outs = refs[SPAN], refs[SPAN + 1 : 2 * SPAN + 1]
    p_ref, dp_ref, sum_ref, turn_ref, acc_ref = refs[2 * SPAN + 1 :]
    h = pl.program_id(0)
    last = pl.num_programs(0) - 1
    peer = peer_ref[0]
    q, do = q_ref[...], do_ref[...]
    lse = lse_ref[0]

    def first(k):
        nt = (((1,), (1,)), ((), ()))
        s = lax.dot_general(pieces[k][:, :HD], q, nt, preferred_element_type=F32)
        p = jnp.exp(s * scale - lse)
        if k == 0:
            p = jnp.where(col_ref[...] <= row_ref[...], p, 0.0)
        dp = lax.dot_general(pieces[k][:, HD:], do, nt, preferred_element_type=F32)
        p_ref[k] = p
        dp_ref[k] = dp
        return jnp.sum(p * dp, axis=0, keepdims=True)

    def second(k):
        p = p_ref[k]
        ds = (p * (dp_ref[k] - sum_ref[...])).astype(BF)
        dk = jnp.dot(ds, q, preferred_element_type=F32)
        dv = jnp.dot(p.astype(BF), do, preferred_element_type=F32)

        @pl.when(h == 0)
        def _():
            acc_ref[k, :, :HD] = dk
            acc_ref[k, :, HD:] = dv

        @pl.when(h > 0)
        def _():
            acc_ref[k, :, :HD] += dk
            acc_ref[k, :, HD:] += dv

        return lax.dot_general(
            pieces[k][:, :HD], ds, (((0,), (0,)), ((), ())), preferred_element_type=F32
        )

    sum_ref[...] = first(0)
    for k in range(1, SPAN):

        @pl.when(peer >= k)
        def _():
            sum_ref[...] += first(k)

    turn_ref[...] = second(0)
    for k in range(1, SPAN):

        @pl.when(peer >= k)
        def _():
            turn_ref[...] += second(k)

    dq = turn_ref[...].T * scale
    dq = dq * cos_ref[...] - pltpu.roll(dq, HD // 2, 1) * sign_ref[...]
    dq_ref[...] = dq.astype(BF)

    @pl.when(h == last)
    def _():
        for k in range(SPAN):

            @pl.when(peer >= k)
            def _():
                outs[k][:, :HD] = (acc_ref[k, :, :HD] * scale).astype(outs[k].dtype)
                outs[k][:, HD:] = acc_ref[k, :, HD:].astype(outs[k].dtype)

            @pl.when(peer < k)
            def _():
                outs[k][...] = jnp.zeros(outs[k].shape, outs[k].dtype)


def attend_back(queries, grads, lse, pieces, peer, order, cosine, signed, heads, scale):
    rows = queries.shape[0]
    full = SPAN * rows
    whole = pl.BlockSpec((rows, 2 * HD), lambda h: (0, 0))
    table = pl.BlockSpec((rows, HD), lambda h: (0, 0))
    one_head = pl.BlockSpec((rows, HD), lambda h: (0, h))
    return pl.pallas_call(
        functools.partial(attend_back_kernel, scale),
        grid=(heads,),
        in_specs=[
            pl.BlockSpec(memory_space=pltpu.SMEM),
            pl.BlockSpec((rows, 1), lambda h: (0, 0)),
            pl.BlockSpec((1, rows), lambda h: (0, 0)),
            table,
            table,
            one_head,
            one_head,
            pl.BlockSpec((1, 1, rows), lambda h: (h, 0, 0)),
            *[whole] * SPAN,
        ],
        out_specs=[one_head, *[whole] * SPAN],
        out_shape=[
            jax.ShapeDtypeStruct((rows, heads * HD), BF),
            jax.ShapeDtypeStruct((rows, 2 * HD), F32),
            *[jax.ShapeDtypeStruct((rows, 2 * HD), BF)] * (SPAN - 1),
        ],
        scratch_shapes=[
            pltpu.VMEM((SPAN, rows, rows), F32),
            pltpu.VMEM((SPAN, rows, rows), F32),
            pltpu.VMEM((1, rows), F32),
            pltpu.VMEM((HD, rows), F32),
            pltpu.VMEM((SPAN, rows, 2 * HD), F32),
        ],
        cost_estimate=pl.CostEstimate(
            flops=10 * heads * rows * full * HD,
            bytes_accessed=4 * rows * HD * (2 * heads + 2 * SPAN),
            transcendentals=heads * rows * full,
        ),
        name="attend_back",
    )(peer, order[:, None], order[None, :], cosine, signed, queries, grads, lse, *pieces)


def step(layer_input, g_out, attn_gain, w_query, w_keyval, w_out, ffn_gain, w_gate, w_up, w_down):
    section = lax.axis_index("section")
    col = lax.axis_index("col")
    peer = lax.axis_index(ROW) % SPAN
    cols = lax.axis_size("col")
    is_first = section == 0
    is_key = col % 2 == 0
    rows = layer_input.shape[2]
    width = layer_input.shape[3]
    own_rows = rows // cols
    full = width * cols
    heads = w_query.shape[2] // HD
    query_cols = w_query.shape[2]
    qkv_cols = query_cols + 2 * HD
    units = w_gate.shape[2]
    scale = 1.0 / math.sqrt(HD)

    def by_section(first, second):
        return jnp.where(is_first, first, second)

    def by_key(first, second):
        return jnp.where(is_key, first, second)

    def xor_rows(block):
        return jnp.concatenate(
            [lax.dynamic_slice_in_dim(block, (col ^ k) * own_rows, own_rows, 0) for k in range(cols)],
            axis=0,
        )

    def reorder(block, k):
        parts = jnp.split(block, cols, axis=0)
        return jnp.concatenate([parts[m ^ k] for m in range(cols)], axis=0)

    def gather_width(block):
        parts = [reorder(part, k) for k, part in enumerate(gather_blocks(xor_rows(block)))]
        total = jnp.zeros((block.shape[0], full), block.dtype)
        for k, part in enumerate(parts):
            total = lax.dynamic_update_slice_in_dim(total, part, (col ^ k) * width, 1)
        return total

    def tokens_from_width(block):
        total = jnp.zeros((own_rows, full), block.dtype)
        for k in range(cols):
            part = lax.dynamic_slice_in_dim(block, (col ^ k) * own_rows, own_rows, 0)
            if k:
                part = over_col(part, k)
            total = lax.dynamic_update_slice_in_dim(total, part, (col ^ k) * width, 1)
        return total

    def width_from_tokens(block):
        total = jnp.zeros((rows, width), block.dtype)
        for k in range(cols):
            part = lax.dynamic_slice_in_dim(block, (col ^ k) * width, width, 1)
            if k:
                part = over_col(part, k)
            total = lax.dynamic_update_slice_in_dim(total, part, (col ^ k) * own_rows, 0)
        return total

    gains_own = jnp.stack([attn_gain[0], ffn_gain[0]])
    gains_other = over_section(gains_own)
    gains_part = jnp.stack([by_section(gains_own, gains_other), by_section(gains_other, gains_own)])
    gains = jnp.zeros((2, 2, full), F32)
    for k in range(cols):
        part = over_col(gains_part, k) if k else gains_part
        gains = lax.dynamic_update_slice_in_dim(gains, part, (col ^ k) * width, 2)

    shard = w_query.shape[1]
    keyval_other = over_col(w_keyval[0], 1)
    attn_own = jnp.concatenate(
        [
            w_query[0],
            by_key(w_keyval[0], keyval_other),
            by_key(keyval_other, w_keyval[0]),
            w_out[0].T,
        ],
        axis=1,
    )
    half_rows = shard // 2
    wide = -(-units // 256) * 256
    half_units = wide // 2

    def both_layers(low, high):
        got = over_section(by_section(high, low))
        return by_section(low, got), by_section(got, high)

    def widen(array):
        return jnp.pad(array, ((0, 0), (0, wide - units)))

    down_own = widen(w_down[0].T)
    attn_parts = both_layers(attn_own[:half_rows], attn_own[half_rows:])
    gate_up_parts = both_layers(widen(w_gate[0]), widen(w_up[0]))
    down_parts = both_layers(down_own[:, :half_units], down_own[:, half_units:])

    def gather_layers(part):
        both = lax.all_gather(part, ("section", ROW), axis=0, tiled=True)
        return both[:full], both[full:]

    def gather_attn(part):
        return lax.all_gather(part, (ROW, "section"), axis=0, tiled=True)

    order = jnp.concatenate(
        [(col ^ k) * own_rows + jnp.arange(own_rows, dtype=jnp.int32) for k in range(cols)]
    )
    positions = peer * rows + order
    cosine, sine = rope_tables(positions, HD)
    signed = jnp.where(jnp.arange(HD) < HD // 2, -sine, sine)

    def swap_halves(values):
        return jnp.concatenate([values[:, HD // 2 :], values[:, : HD // 2]], axis=1)

    peers = jnp.reshape(peer, (1,)).astype(jnp.int32)

    def attn_forward(normed, attn_w):
        queries, key_value = project_turn(normed, attn_w, cosine, signed, heads)
        pieces = [key_value] + [along_row(key_value, k) for k in range(1, SPAN)]
        attended, lse = attend(queries, pieces, peers, order, heads, scale)
        return attended, (normed, queries, pieces, lse, attended)

    def attn_out(resid, attended, attn_w):
        return resid + scatter_tokens(dot(attended, attn_w[:, qkv_cols:], 1, 1).astype(BF))

    def ffn_gather(middle, ffn_gain):
        normed_own, inverse_ffn = norm(middle, ffn_gain)
        return gather_tokens(normed_own), inverse_ffn

    def ffn_in(normed_ffn, gate_up_w):
        gate = dot(normed_ffn, gate_up_w[0], 1, 0)
        up = dot(normed_ffn, gate_up_w[1], 1, 0)
        return gate.astype(BF), up.astype(BF), (jax.nn.silu(gate) * up).astype(BF)

    def ffn_out(hidden, down_w):
        out = dot(hidden[:, :half_units], down_w[0], 1, 1)
        return scatter_tokens((out + dot(hidden[:, half_units:], down_w[1], 1, 1)).astype(BF))

    def swap_add(left, first, second):
        got = over_section(dot(left, by_section(second, first), 0, 0).astype(BF))
        return (dot(left, by_section(first, second), 0, 0) + got.astype(F32)).astype(BF)

    def scatter_rows(total):
        return lax.psum_scatter(total, ROW, scatter_dimension=0, tiled=True)

    def ffn_backward(grad_own, grad_branch, kept, ffn_gain, gate_up_w, down_w):
        middle, inverse_ffn, normed_ffn, gate, up, hidden = kept
        down_total = swap_add(grad_branch, hidden[:, :half_units], hidden[:, half_units:])
        grad_branch, down_total = after(grad_branch, down_total)
        down_sum = scatter_rows(down_total)
        grad_hidden = jnp.concatenate(
            [dot(grad_branch, down_w[0], 1, 0), dot(grad_branch, down_w[1], 1, 0)], axis=1
        )
        gate, up = gate.astype(F32), up.astype(F32)
        sigma = jax.nn.sigmoid(gate)
        dgate = (grad_hidden * up * sigma * (1.0 + gate * (1.0 - sigma))).astype(BF)
        dup = (grad_hidden * gate * sigma).astype(BF)
        grad_normed_ffn = scatter_tokens(
            (dot(dgate, gate_up_w[0], 1, 1) + dot(dup, gate_up_w[1], 1, 1)).astype(BF)
        )
        gate_up_total = swap_add(normed_ffn, dgate, dup)
        grad_normed_ffn, gate_up_total = after(grad_normed_ffn, gate_up_total)
        gate_up_sum = scatter_rows(gate_up_total)
        grad_middle, grad_gain_ffn = norm_backward(grad_normed_ffn, middle, inverse_ffn, ffn_gain)
        return grad_own + grad_middle, gate_up_sum, down_sum, grad_gain_ffn

    def attn_backward(grad_middle, resid, inverse_attn, kept, attn_gain, attn_w, *others):
        normed, queries, pieces, lse, attended = kept
        w_qkv, w_o = attn_w[:, :qkv_cols], attn_w[:, qkv_cols:]
        grad_attn_out = gather_tokens(grad_middle.astype(BF))
        grad_attended = dot(grad_attn_out, w_o, 1, 0).astype(BF)
        grad_query_raw, grad_mine, *grad_sent = attend_back(
            queries, grad_attended, lse, pieces, peers, order, cosine, signed, heads, scale
        )
        for k in range(1, SPAN):
            grad_mine = grad_mine + along_row(grad_sent[k - 1], -k).astype(F32)
        grad_wout = dot(grad_attn_out, attended, 0, 0).astype(BF)
        grad_wquery = dot(normed, grad_query_raw, 0, 0).astype(BF)
        got = over_section(by_section(grad_wout, grad_wquery))
        early = by_section(grad_wquery, grad_wout).astype(F32) + got.astype(F32)
        grad_mine, early, *others = after(grad_mine, early.astype(BF), *others)
        early = scatter_rows(early)
        grad_key = grad_mine[:, :HD]
        grad_keyval = jnp.concatenate(
            [
                (grad_key * cosine - swap_halves(grad_key) * signed).astype(BF),
                grad_mine[:, HD:].astype(BF),
            ],
            axis=1,
        )
        grad_wkeyval = dot(normed, grad_keyval, 0, 0).astype(BF)
        grad_wkey, grad_wvalue = grad_wkeyval[:, :HD], grad_wkeyval[:, HD:]
        got = over_section(by_section(grad_wvalue, grad_wkey))
        late = by_section(grad_wkey, grad_wvalue).astype(F32) + got.astype(F32)
        late = late.astype(BF)
        grad_normed = (
            dot(grad_query_raw, w_qkv[:, :query_cols], 1, 1)
            + dot(grad_keyval, w_qkv[:, query_cols:], 1, 1)
        ).astype(BF)
        grad_normed = scatter_tokens(grad_normed)
        grad_resid, grad_gain_attn = norm_backward(grad_normed, resid, inverse_attn, attn_gain)
        return grad_middle + grad_resid, early, late, grad_gain_attn, others

    def own_width(block):
        block = lax.dynamic_slice_in_dim(block, col * width, width, 1)
        return xor_rows(block)

    def core_swap(layer, block):
        return block, lax.ppermute(block, "section", [(1 - layer, layer)])

    def by_layer(first, second):
        first, first_got = first
        second, second_got = second
        return jnp.stack([by_section(first, second_got), by_section(first_got, second)])

    def to_core(layer, block):
        got = lax.ppermute(block, "section", [(1 - layer, layer)])
        return (block, got) if layer == 0 else (got, block)

    attn_w = [gather_attn(attn_parts[0])]
    x_full = gather_width(lax.dynamic_index_in_dim(layer_input[:, 0], section, 0, keepdims=False))
    gate_up_w = [gather_layers(gate_up_parts[0])]
    normed, inverse = norm(x_full.astype(F32), gains[0, 0])
    resid_0, inverse_0 = x_full[:own_rows].astype(F32), inverse[:own_rows]
    _, down_part = after(normed, down_parts[0])
    down_w = [gather_layers(down_part)]
    attended, kept_attn_0 = attn_forward(normed, attn_w[0])
    _, attn_part = after(attended, attn_parts[1])
    attn_w.append(gather_attn(attn_part))
    middle = attn_out(resid_0, attended, attn_w[0])
    _, gate_up_part = after(middle, gate_up_parts[1])
    gate_up_w.append(gather_layers(gate_up_part))
    normed_ffn, inverse_ffn = ffn_gather(middle, gains[0, 1])
    gate, up, hidden = ffn_in(normed_ffn, gate_up_w[0])
    _, down_part = after(hidden, down_parts[1])
    down_w.append(gather_layers(down_part))
    result = middle + ffn_out(hidden, down_w[0])
    kept_ffn_0 = (middle, inverse_ffn, normed_ffn, gate, up, hidden)
    x_full = gather_tokens(result.astype(BF))
    act_0 = core_swap(0, own_width(x_full))
    normed, inverse = norm(x_full.astype(F32), gains[1, 0])
    resid_1, inverse_1 = x_full[:own_rows].astype(F32), inverse[:own_rows]
    attended, kept_attn_1 = attn_forward(normed, attn_w[1])
    _, g_out = after(attended, g_out)
    middle = attn_out(resid_1, attended, attn_w[1])
    normed_ffn, inverse_ffn = ffn_gather(middle, gains[1, 1])
    top = lax.dynamic_index_in_dim(g_out[:, 0], section, 0, keepdims=False)
    top_branch = gather_width(top.astype(BF))
    top_own = tokens_from_width(top)
    gate, up, hidden = ffn_in(normed_ffn, gate_up_w[1])
    result = middle + ffn_out(hidden, down_w[1])
    kept_ffn_1 = (middle, inverse_ffn, normed_ffn, gate, up, hidden)
    act_1 = core_swap(1, width_from_tokens(result.astype(BF)))
    acts = by_layer(act_0, act_1)

    grad_middle, gate_up_1, down_1, gain_ffn_1 = ffn_backward(
        top_own, top_branch, kept_ffn_1, gains[1, 1], gate_up_w[1], down_w[1]
    )
    grad_1, early_1, late_1, gain_attn_1, (acts,) = attn_backward(
        grad_middle, resid_1, inverse_1, kept_attn_1, gains[1, 0], attn_w[1], acts
    )
    grad_1 = grad_1.astype(BF)
    branch, late_1 = after(gather_tokens(grad_1), late_1)
    late_1 = scatter_rows(late_1)
    grads_1 = core_swap(1, own_width(branch))
    grad_middle, gate_up_0, down_0, gain_ffn_0 = ffn_backward(
        grad_1.astype(F32), branch, kept_ffn_0, gains[0, 1], gate_up_w[0], down_w[0]
    )
    grad_0, early_0, late_0, gain_attn_0, _ = attn_backward(
        grad_middle, resid_0, inverse_0, kept_attn_0, gains[0, 0], attn_w[0]
    )
    grads_in = by_layer(core_swap(0, width_from_tokens(grad_0.astype(BF))), grads_1)
    late_0 = scatter_rows(late_0)

    def own_layer(first, second):
        return jax.tree.map(by_section, tuple(first), tuple(second))

    def final(zero, one):
        return own_layer(to_core(0, zero), to_core(1, one))

    final_query, final_out = final(early_0, early_1)
    final_key, final_value = final(late_0, late_1)
    final_keyval = by_key(final_key, final_value).astype(F32) + over_col(
        by_key(final_value, final_key), 1
    ).astype(F32)
    final_gate, final_up = final(gate_up_0, gate_up_1)
    final_down = jnp.concatenate(final(down_0, down_1), axis=1)[:, :units]

    gain_grads_0 = jnp.stack([gain_attn_0, gain_ffn_0])
    gain_grads_1 = jnp.stack([gain_attn_1, gain_ffn_1])
    gain_sums = by_section(gain_grads_0, gain_grads_1) + over_section(
        by_section(gain_grads_1, gain_grads_0)
    )
    gain_parts = [
        lax.dynamic_slice_in_dim(gain_sums, (col ^ k) * width, width, 1) for k in range(cols)
    ]
    gain_sums = gain_parts[0] + sum(over_col(gain_parts[k], k) for k in range(1, cols))
    row_count = lax.axis_size(ROW)
    step = 1
    while step < row_count:
        gain_sums = gain_sums + lax.ppermute(
            gain_sums, ROW, [(i, i ^ step) for i in range(row_count)]
        )
        step *= 2

    return (
        acts.reshape(1, 2, 1, rows, width),
        grads_in.reshape(1, 2, 1, rows, width),
        gain_sums[:1],
        final_query[None].astype(F32),
        final_keyval[None],
        final_out.T[None].astype(F32),
        gain_sums[1:],
        final_gate[None, :, :units].astype(F32),
        final_up[None, :, :units].astype(F32),
        final_down.astype(F32).T[None],
    )


def solution(mesh):
    tokens = P(None, ROW, None, "col")
    gain = P("section", "col")
    rows_cols = P("section", ROW, "col")
    cols_rows = P("section", "col", ROW)
    layers = P("section", None, ROW, None, "col")
    return jax.shard_map(
        step,
        mesh=mesh,
        in_specs=(
            tokens,
            tokens,
            gain,
            rows_cols,
            rows_cols,
            cols_rows,
            gain,
            rows_cols,
            rows_cols,
            cols_rows,
        ),
        out_specs=(
            layers,
            layers,
            gain,
            rows_cols,
            rows_cols,
            cols_rows,
            gain,
            rows_cols,
            rows_cols,
            cols_rows,
        ),
        check_vma=False,
    )
```

```python
import functools
import math

import jax
import jax.numpy as jnp
from jax import lax
from jax.experimental import pallas as pl
from jax.experimental.pallas import tpu as pltpu
from jax.sharding import PartitionSpec as P


HD = 128
SPAN = 4
EPS = 1e-06
THETA = 1000000.0
BF = jnp.bfloat16
F32 = jnp.float32


def dot(left, right, left_dim, right_dim):
    return lax.dot_general(
        left, right, (((left_dim,), (right_dim,)), ((), ())), preferred_element_type=F32
    )


def rope_tables(positions, head_size):
    half = head_size // 2
    freqs = THETA ** (-(jnp.arange(half, dtype=F32) * 2.0) / head_size)
    angles = positions.astype(F32)[:, None] * freqs[None, :]
    angles = jnp.concatenate([angles, angles], axis=-1)
    return (jnp.cos(angles), jnp.sin(angles))


ROW = "row"


def after(value, *others):
    return lax.optimization_barrier((value, *others))


def over_col(block, step):
    count = lax.axis_size("col")
    return lax.ppermute(block, "col", [(i, i ^ step) for i in range(count)])


def over_section(block):
    return lax.ppermute(block, "section", [(0, 1), (1, 0)])


def along_row(block, steps):
    count = lax.axis_size(ROW)
    route = [(i, i + steps) for i in range(count) if 0 <= i % SPAN + steps < SPAN]
    return lax.ppermute(block, ROW, route)


def gather_blocks(own):
    half = own.shape[0] // 2
    first = over_col(own, 1)
    second = over_col(own, 2)
    third_low = over_col(first[:half], 2)
    third_high = over_col(second[half:], 1)
    return own, first, second, jnp.concatenate([third_low, third_high], axis=0)


def gather_tokens(own):
    return jnp.concatenate(gather_blocks(own), axis=0)


def scatter_tokens(partial):
    blocks = jnp.split(partial, 4, axis=0)
    got = [over_col(blocks[k], k).astype(F32) for k in (3, 1, 2)]
    return blocks[0].astype(F32) + got[0] + got[1] + got[2]


def norm(resid, gain):
    inverse = lax.rsqrt(jnp.mean(resid * resid, axis=1, keepdims=True) + EPS)
    return (resid * inverse * gain[None, :]).astype(BF), inverse


def norm_backward(grad_normed, resid, inverse, gain):
    scaled = resid * inverse
    grad_gain = jnp.sum(grad_normed * scaled, axis=0)
    grad_scaled = grad_normed * gain[None, :]
    mean_term = jnp.mean(grad_scaled * scaled, axis=1, keepdims=True)
    return inverse * (grad_scaled - scaled * mean_term), grad_gain


def qkv_kernel(heads, x_ref, w_ref, cos_ref, sign_ref, own_cos_ref, own_sign_ref, q_ref, own_ref):
    raw = jnp.dot(x_ref[...], w_ref[...], preferred_element_type=F32)
    for h in range(heads + 1):
        z = raw[:, h * HD : (h + 1) * HD]
        if h < heads:
            z = z * cos_ref[...] + pltpu.roll(z, HD // 2, 1) * sign_ref[...]
            q_ref[:, h * HD : (h + 1) * HD] = z.astype(BF)
        else:
            z = z * own_cos_ref[...] + pltpu.roll(z, HD // 2, 1) * own_sign_ref[...]
            own_ref[...] = z.astype(BF)


def project_turn(normed, weight, tables, heads):
    rows, depth = normed.shape
    step = rows // 2
    cols = (heads + 1) * HD
    table = pl.BlockSpec((step, HD), lambda i: (i, 0))
    return pl.pallas_call(
        functools.partial(qkv_kernel, heads),
        grid=(2,),
        in_specs=[
            pl.BlockSpec((step, depth), lambda i: (i, 0)),
            pl.BlockSpec((depth, cols), lambda i: (0, 0)),
            *[table] * 4,
        ],
        out_specs=[
            pl.BlockSpec((step, heads * HD), lambda i: (i, 0)),
            pl.BlockSpec((step, HD), lambda i: (i, 0)),
        ],
        out_shape=[
            jax.ShapeDtypeStruct((rows, heads * HD), BF),
            jax.ShapeDtypeStruct((rows, HD), BF),
        ],
        cost_estimate=pl.CostEstimate(
            flops=2 * rows * depth * cols,
            bytes_accessed=2 * (rows * depth + depth * cols + rows * cols),
            transcendentals=0,
        ),
        name="project_turn",
    )(normed, weight, *tables)


def swapped(k, rows):
    quarter = rows // 4
    return [
        (pl.ds(k * rows + i * quarter, quarter), pl.ds((i ^ 1) * quarter, quarter)) for i in range(4)
    ]


def attend_kernel(scale, flag_ref, col_ref, row_ref, q_ref, *refs):
    mine, theirs = refs[:SPAN], refs[SPAN : 2 * SPAN]
    o_ref, lse_ref, k_ref, v_ref, e_ref, total_ref, acc_ref = refs[2 * SPAN :]
    rows = q_ref.shape[0]
    peer, is_key = flag_ref[0], flag_ref[1]
    q = q_ref[...]

    def place(own_ref, other_ref):
        for k in range(SPAN):
            own_ref[k * rows : (k + 1) * rows] = mine[k][...]
            for here, there in swapped(k, rows):
                other_ref[here] = theirs[k][there]

    @pl.when((pl.program_id(0) == 0) & (is_key == 1))
    def _():
        place(k_ref, v_ref)

    @pl.when((pl.program_id(0) == 0) & (is_key == 0))
    def _():
        place(v_ref, k_ref)

    def piece(ref, k):
        return ref[k * rows : (k + 1) * rows]

    def exps(k):
        s = lax.dot_general(
            piece(k_ref, k), q, (((1,), (1,)), ((), ())), preferred_element_type=F32
        )
        return jnp.exp(s * scale)

    e = jnp.where(col_ref[...] <= row_ref[...], exps(0), 0.0)
    e_ref[0] = e
    total_ref[...] = jnp.sum(e, axis=0, keepdims=True)
    for k in range(1, SPAN):

        @pl.when(peer >= k)
        def _():
            e = exps(k)
            e_ref[k] = e
            total_ref[...] += jnp.sum(e, axis=0, keepdims=True)

    total = total_ref[...]
    lse_ref[0] = jnp.log(total)
    shrink = jnp.where(total > 1.0, 2.0**-64, 1.0)
    inverse = 1.0 / (total * shrink)

    def term(k):
        p = ((e_ref[k] * shrink) * inverse).astype(BF)
        return lax.dot_general(
            piece(v_ref, k), p, (((0,), (0,)), ((), ())), preferred_element_type=F32
        )

    acc_ref[...] = term(0)
    for k in range(1, SPAN):

        @pl.when(peer >= k)
        def _():
            acc_ref[...] += term(k)

    o_ref[...] = acc_ref[...].T.astype(BF)


def attend(queries, mine, first, later, flags, order, heads, scale):
    rows = queries.shape[0]
    full = SPAN * rows
    piece = pl.BlockSpec((rows, HD), lambda h: (0, 0))
    whole = pl.BlockSpec((full, HD), lambda h: (0, 0))
    return pl.pallas_call(
        functools.partial(attend_kernel, scale),
        grid=(heads,),
        in_specs=[
            pl.BlockSpec(memory_space=pltpu.SMEM),
            pl.BlockSpec((rows, 1), lambda h: (0, 0)),
            pl.BlockSpec((1, rows), lambda h: (0, 0)),
            pl.BlockSpec((rows, HD), lambda h: (0, h)),
            *[piece] * SPAN,
            piece,
            *[pl.BlockSpec((rows, HD), lambda h, k=k: (k, 0)) for k in range(SPAN - 1)],
        ],
        out_specs=[
            pl.BlockSpec((rows, HD), lambda h: (0, h)),
            pl.BlockSpec((1, 1, rows), lambda h: (h, 0, 0)),
            whole,
            whole,
        ],
        out_shape=[
            jax.ShapeDtypeStruct((rows, heads * HD), BF),
            jax.ShapeDtypeStruct((heads, 1, rows), F32),
            jax.ShapeDtypeStruct((full, HD), BF),
            jax.ShapeDtypeStruct((full, HD), BF),
        ],
        scratch_shapes=[
            pltpu.VMEM((SPAN, rows, rows), F32),
            pltpu.VMEM((1, rows), F32),
            pltpu.VMEM((HD, rows), F32),
        ],
        cost_estimate=pl.CostEstimate(
            flops=4 * heads * rows * full * HD,
            bytes_accessed=4 * rows * HD * (heads + 2 * SPAN),
            transcendentals=heads * rows * full,
        ),
        name="attend",
    )(flags, order[:, None], order[None, :], queries, *mine, first, *[later] * (SPAN - 1))


def attend_back_kernel(
    scale, flag_ref, col_ref, row_ref, cos_ref, sign_ref, q_ref, do_ref, lse_ref, k_ref, v_ref,
    dq_ref, keep_ref, send_ref, p_ref, dp_ref, sum_ref, turn_ref, dk_ref, dv_ref,
):
    h = pl.program_id(0)
    last = pl.num_programs(0) - 1
    rows = q_ref.shape[0]
    peer, is_key = flag_ref[0], flag_ref[1]
    q, do = q_ref[...], do_ref[...]
    lse = lse_ref[0]

    def piece(ref, k):
        return ref[k * rows : (k + 1) * rows]

    def first(k):
        nt = (((1,), (1,)), ((), ()))
        s = lax.dot_general(piece(k_ref, k), q, nt, preferred_element_type=F32)
        p = jnp.exp(s * scale - lse)
        if k == 0:
            p = jnp.where(col_ref[...] <= row_ref[...], p, 0.0)
        dp = lax.dot_general(piece(v_ref, k), do, nt, preferred_element_type=F32)
        p_ref[k] = p
        dp_ref[k] = dp
        return jnp.sum(p * dp, axis=0, keepdims=True)

    def second(k):
        p = p_ref[k]
        ds = (p * (dp_ref[k] - sum_ref[...])).astype(BF)
        dk = jnp.dot(ds, q, preferred_element_type=F32)
        dv = jnp.dot(p.astype(BF), do, preferred_element_type=F32)

        @pl.when(h == 0)
        def _():
            dk_ref[k * rows : (k + 1) * rows] = dk
            dv_ref[k * rows : (k + 1) * rows] = dv

        @pl.when(h > 0)
        def _():
            dk_ref[k * rows : (k + 1) * rows] += dk
            dv_ref[k * rows : (k + 1) * rows] += dv

        return lax.dot_general(
            piece(k_ref, k), ds, (((0,), (0,)), ((), ())), preferred_element_type=F32
        )

    sum_ref[...] = first(0)
    for k in range(1, SPAN):

        @pl.when(peer >= k)
        def _():
            sum_ref[...] += first(k)

    turn_ref[...] = second(0)
    for k in range(1, SPAN):

        @pl.when(peer >= k)
        def _():
            turn_ref[...] += second(k)

        @pl.when((peer < k) & (h == 0))
        def _():
            dk_ref[k * rows : (k + 1) * rows] = jnp.zeros((rows, HD), F32)
            dv_ref[k * rows : (k + 1) * rows] = jnp.zeros((rows, HD), F32)

    dq = turn_ref[...].T * scale
    dq = dq * cos_ref[...] - pltpu.roll(dq, HD // 2, 1) * sign_ref[...]
    dq_ref[...] = dq.astype(BF)

    @pl.when((h == last) & (is_key == 1))
    def _():
        keep_ref[...] = dk_ref[...] * scale
        for k in range(SPAN):
            for here, there in swapped(k, rows):
                to = pl.ds(k * rows + there.start, there.size)
                send_ref[to] = dv_ref[here].astype(BF)

    @pl.when((h == last) & (is_key == 0))
    def _():
        keep_ref[...] = dv_ref[...]
        for k in range(SPAN):
            for here, there in swapped(k, rows):
                to = pl.ds(k * rows + there.start, there.size)
                send_ref[to] = (dk_ref[here] * scale).astype(BF)


def attend_back(queries, grads, lse, keys, values, flags, order, cosine, signed, heads, scale):
    rows = queries.shape[0]
    full = SPAN * rows
    whole = pl.BlockSpec((full, HD), lambda h: (0, 0))
    table = pl.BlockSpec((rows, HD), lambda h: (0, 0))
    one_head = pl.BlockSpec((rows, HD), lambda h: (0, h))
    return pl.pallas_call(
        functools.partial(attend_back_kernel, scale),
        grid=(heads,),
        in_specs=[
            pl.BlockSpec(memory_space=pltpu.SMEM),
            pl.BlockSpec((rows, 1), lambda h: (0, 0)),
            pl.BlockSpec((1, rows), lambda h: (0, 0)),
            table,
            table,
            one_head,
            one_head,
            pl.BlockSpec((1, 1, rows), lambda h: (h, 0, 0)),
            whole,
            whole,
        ],
        out_specs=[one_head, whole, whole],
        out_shape=[
            jax.ShapeDtypeStruct((rows, heads * HD), BF),
            jax.ShapeDtypeStruct((full, HD), F32),
            jax.ShapeDtypeStruct((full, HD), BF),
        ],
        scratch_shapes=[
            pltpu.VMEM((SPAN, rows, rows), F32),
            pltpu.VMEM((SPAN, rows, rows), F32),
            pltpu.VMEM((1, rows), F32),
            pltpu.VMEM((HD, rows), F32),
            pltpu.VMEM((full, HD), F32),
            pltpu.VMEM((full, HD), F32),
        ],
        cost_estimate=pl.CostEstimate(
            flops=10 * heads * rows * full * HD,
            bytes_accessed=4 * rows * HD * (2 * heads + 2 * SPAN),
            transcendentals=heads * rows * full,
        ),
        name="attend_back",
    )(flags, order[:, None], order[None, :], cosine, signed, queries, grads, lse, keys, values)


def step(layer_input, g_out, attn_gain, w_query, w_keyval, w_out, ffn_gain, w_gate, w_up, w_down):
    section = lax.axis_index("section")
    col = lax.axis_index("col")
    peer = lax.axis_index(ROW) % SPAN
    cols = lax.axis_size("col")
    is_first = section == 0
    is_key = col % 2 == 0
    rows = layer_input.shape[2]
    width = layer_input.shape[3]
    own_rows = rows // cols
    full = width * cols
    heads = w_query.shape[2] // HD
    query_cols = w_query.shape[2]
    qkv_cols = query_cols + HD
    units = w_gate.shape[2]
    scale = 1.0 / math.sqrt(HD)

    def by_section(first, second):
        return jnp.where(is_first, first, second)

    def by_key(first, second):
        return jnp.where(is_key, first, second)

    def xor_rows(block):
        return jnp.concatenate(
            [lax.dynamic_slice_in_dim(block, (col ^ k) * own_rows, own_rows, 0) for k in range(cols)],
            axis=0,
        )

    def reorder(block, k):
        parts = jnp.split(block, cols, axis=0)
        return jnp.concatenate([parts[m ^ k] for m in range(cols)], axis=0)

    def gather_width(block):
        parts = [reorder(part, k) for k, part in enumerate(gather_blocks(xor_rows(block)))]
        total = jnp.zeros((block.shape[0], full), block.dtype)
        for k, part in enumerate(parts):
            total = lax.dynamic_update_slice_in_dim(total, part, (col ^ k) * width, 1)
        return total

    def tokens_from_width(block):
        total = jnp.zeros((own_rows, full), block.dtype)
        for k in range(cols):
            part = lax.dynamic_slice_in_dim(block, (col ^ k) * own_rows, own_rows, 0)
            if k:
                part = over_col(part, k)
            total = lax.dynamic_update_slice_in_dim(total, part, (col ^ k) * width, 1)
        return total

    def width_from_tokens(block):
        total = jnp.zeros((rows, width), block.dtype)
        for k in range(cols):
            part = lax.dynamic_slice_in_dim(block, (col ^ k) * width, width, 1)
            if k:
                part = over_col(part, k)
            total = lax.dynamic_update_slice_in_dim(total, part, (col ^ k) * own_rows, 0)
        return total

    gains_own = jnp.stack([attn_gain[0], ffn_gain[0]])
    gains_other = over_section(gains_own)
    gains_part = jnp.stack([by_section(gains_own, gains_other), by_section(gains_other, gains_own)])
    gains = jnp.zeros((2, 2, full), F32)
    for k in range(cols):
        part = over_col(gains_part, k) if k else gains_part
        gains = lax.dynamic_update_slice_in_dim(gains, part, (col ^ k) * width, 2)

    shard = w_query.shape[1]
    attn_own = jnp.concatenate([w_query[0], w_keyval[0], w_out[0].T], axis=1)
    half_rows = shard // 2
    wide = -(-units // 256) * 256
    half_units = wide // 2

    def both_layers(low, high):
        got = over_section(by_section(high, low))
        return by_section(low, got), by_section(got, high)

    def widen(array):
        return jnp.pad(array, ((0, 0), (0, wide - units)))

    down_own = widen(w_down[0].T)
    attn_parts = both_layers(attn_own[:half_rows], attn_own[half_rows:])
    gate_up_parts = both_layers(widen(w_gate[0]), widen(w_up[0]))
    down_parts = both_layers(down_own[:, :half_units], down_own[:, half_units:])

    def gather_layers(part):
        return lax.all_gather(part, ("section", ROW), axis=0, tiled=True)

    def split_layers(both):
        return both[:full], both[full:]

    def gather_attn(part):
        return lax.all_gather(part, (ROW, "section"), axis=0, tiled=True)

    order = jnp.concatenate(
        [(col ^ k) * own_rows + jnp.arange(own_rows, dtype=jnp.int32) for k in range(cols)]
    )
    positions = peer * rows + order
    cosine, sine = rope_tables(positions, HD)
    signed = jnp.where(jnp.arange(HD) < HD // 2, -sine, sine)

    def swap_halves(values):
        return jnp.concatenate([values[:, HD // 2 :], values[:, : HD // 2]], axis=1)

    flags = jnp.stack([peer, jnp.where(is_key, 1, 0)]).astype(jnp.int32)
    own_cosine = by_key(cosine, jnp.ones_like(cosine))
    own_signed = by_key(signed, jnp.zeros_like(signed))
    tables = (cosine, signed, own_cosine, own_signed)

    def attn_forward(normed, attn_w):
        queries, own = project_turn(normed, attn_w, tables, heads)
        first = over_col(own, 1)
        mine = [own] + [along_row(own, k) for k in range(1, SPAN)]
        later = over_col(jnp.concatenate(mine[1:], axis=0), 1)
        attended, lse, keys, values = attend(
            queries, mine, first, later, flags, order, heads, scale
        )
        return attended, (normed, queries, keys, values, lse, attended)

    def attn_out(resid, attended, attn_w):
        return resid + scatter_tokens(dot(attended, attn_w[:, qkv_cols:], 1, 1).astype(BF))

    def ffn_gather(middle, ffn_gain):
        normed_own, inverse_ffn = norm(middle, ffn_gain)
        return gather_tokens(normed_own), inverse_ffn

    def ffn_in(normed_ffn, gate_up_w):
        gate_up_w = split_layers(gate_up_w)
        gate = dot(normed_ffn, gate_up_w[0], 1, 0)
        up = dot(normed_ffn, gate_up_w[1], 1, 0)
        return gate.astype(BF), up.astype(BF), (jax.nn.silu(gate) * up).astype(BF)

    def ffn_out(hidden, down_w):
        down_w = split_layers(down_w)
        out = dot(hidden[:, :half_units], down_w[0], 1, 1)
        return scatter_tokens((out + dot(hidden[:, half_units:], down_w[1], 1, 1)).astype(BF))

    def swap_add(left, first, second):
        got = over_section(dot(left, by_section(second, first), 0, 0).astype(BF))
        return (dot(left, by_section(first, second), 0, 0) + got.astype(F32)).astype(BF)

    def scatter_rows(total):
        return lax.psum_scatter(total, ROW, scatter_dimension=0, tiled=True)

    def down_grad(grad_branch, hidden):
        return swap_add(grad_branch, hidden[:, :half_units], hidden[:, half_units:])

    def ffn_backward(layer, grad_own, grad_branch, down_total, kept, ffn_gain, gate_up_w, down_w):
        middle, inverse_ffn, normed_ffn, gate, up = kept
        gate_up_w, down_w = split_layers(gate_up_w), split_layers(down_w)
        down_sum = scatter_rows(down_total)
        grad_hidden = jnp.concatenate(
            [dot(grad_branch, down_w[0], 1, 0), dot(grad_branch, down_w[1], 1, 0)], axis=1
        )
        gate, up = gate.astype(F32), up.astype(F32)
        sigma = jax.nn.sigmoid(gate)
        dgate = (grad_hidden * up * sigma * (1.0 + gate * (1.0 - sigma))).astype(BF)
        dup = (grad_hidden * gate * sigma).astype(BF)
        gate_up_total = swap_add(normed_ffn, dgate, dup)
        if layer == 0:
            dgate, dup, gate_up_total = after(dgate, dup, gate_up_total)
        grad_normed_ffn = (dot(dgate, gate_up_w[0], 1, 1) + dot(dup, gate_up_w[1], 1, 1)).astype(BF)
        grad_normed_ffn = scatter_tokens(grad_normed_ffn)
        if layer == 1:
            grad_normed_ffn, gate_up_total = after(grad_normed_ffn, gate_up_total)
        gate_up_sum = scatter_rows(gate_up_total)
        grad_middle, grad_gain_ffn = norm_backward(grad_normed_ffn, middle, inverse_ffn, ffn_gain)
        grad_middle = grad_own + grad_middle
        return grad_middle, gate_up_sum, down_sum, grad_gain_ffn

    def attn_backward(grad_middle, resid, inverse_attn, kept, attn_gain, attn_w, *others):
        normed, queries, keys, values, lse, attended = kept
        w_qkv, w_o = attn_w[:, :qkv_cols], attn_w[:, qkv_cols:]
        grad_attn_out = gather_tokens(grad_middle.astype(BF))
        grad_attended = dot(grad_attn_out, w_o, 1, 0).astype(BF)
        grad_query_raw, grad_keep, grad_send = attend_back(
            queries, grad_attended, lse, keys, values, flags, order, cosine, signed, heads, scale
        )
        grad_keep = grad_keep + over_col(grad_send, 1).astype(F32)
        pieces = jnp.split(grad_keep, SPAN, axis=0)
        grad_mine = pieces[0]
        for k in range(1, SPAN):
            grad_mine = grad_mine + along_row(pieces[k].astype(BF), -k).astype(F32)
        grad_wout = dot(grad_attn_out, attended, 0, 0).astype(BF)
        grad_wquery = dot(normed, grad_query_raw, 0, 0).astype(BF)
        got = over_section(by_section(grad_wout, grad_wquery))
        early = by_section(grad_wquery, grad_wout).astype(F32) + got.astype(F32)
        grad_mine, early, *others = after(grad_mine, early.astype(BF), *others)
        grad_keyval = grad_mine * own_cosine - swap_halves(grad_mine) * own_signed
        grad_keyval = grad_keyval.astype(BF)
        late = dot(normed, grad_keyval, 0, 0).astype(BF)
        late = late.astype(F32) + over_section(late).astype(F32)
        total = jnp.concatenate([early, late.astype(BF)], axis=1)
        grad_normed = (
            dot(grad_query_raw, w_qkv[:, :query_cols], 1, 1)
            + dot(grad_keyval, w_qkv[:, query_cols:], 1, 1)
        ).astype(BF)
        grad_normed, total = after(scatter_tokens(grad_normed), total)
        attn_sum = scatter_rows(total)
        grad_resid, grad_gain_attn = norm_backward(grad_normed, resid, inverse_attn, attn_gain)
        grad_resid = grad_middle + grad_resid
        return grad_resid, attn_sum, grad_gain_attn, others

    def own_width(block):
        block = lax.dynamic_slice_in_dim(block, col * width, width, 1)
        return xor_rows(block)

    def core_swap(layer, block):
        return block, lax.ppermute(block, "section", [(1 - layer, layer)])

    def by_layer(first, second):
        first, first_got = first
        second, second_got = second
        return jnp.stack([by_section(first, second_got), by_section(first_got, second)])

    def to_core(layer, block):
        got = lax.ppermute(block, "section", [(1 - layer, layer)])
        return (block, got) if layer == 0 else (got, block)

    attn_w = [gather_attn(attn_parts[0])]
    x_full = gather_width(lax.dynamic_index_in_dim(layer_input[:, 0], section, 0, keepdims=False))
    gate_up_w = [gather_layers(gate_up_parts[0])]
    normed, inverse = norm(x_full.astype(F32), gains[0, 0])
    resid_0, inverse_0 = x_full[:own_rows].astype(F32), inverse[:own_rows]
    _, down_part = after(normed, down_parts[0])
    down_w = [gather_layers(down_part)]
    attended, kept_attn_0 = attn_forward(normed, attn_w[0])
    _, attn_part = after(attended, attn_parts[1])
    attn_w.append(gather_attn(attn_part))
    middle = attn_out(resid_0, attended, attn_w[0])
    _, gate_up_part = after(middle, gate_up_parts[1])
    gate_up_w.append(gather_layers(gate_up_part))
    normed_ffn, inverse_ffn = ffn_gather(middle, gains[0, 1])
    gate, up, hidden = ffn_in(normed_ffn, gate_up_w[0])
    _, down_part = after(hidden, down_parts[1])
    down_w.append(gather_layers(down_part))
    result = middle + ffn_out(hidden, down_w[0])
    kept_ffn_0 = (middle, inverse_ffn, normed_ffn, gate, up)
    hidden_0 = hidden
    x_full = gather_tokens(result.astype(BF))
    act_0 = core_swap(0, own_width(x_full))
    normed, inverse = norm(x_full.astype(F32), gains[1, 0])
    resid_1, inverse_1 = x_full[:own_rows].astype(F32), inverse[:own_rows]
    attended, kept_attn_1 = attn_forward(normed, attn_w[1])
    _, g_out = after(attended, g_out)
    middle = attn_out(resid_1, attended, attn_w[1])
    normed_ffn, inverse_ffn = ffn_gather(middle, gains[1, 1])
    top = lax.dynamic_index_in_dim(g_out[:, 0], section, 0, keepdims=False)
    top_branch = gather_width(top.astype(BF))
    top_own = tokens_from_width(top)
    gate, up, hidden = ffn_in(normed_ffn, gate_up_w[1])
    down_w[1], down_total, top_own = after(down_w[1], down_grad(top_branch, hidden), top_own)
    result = middle + ffn_out(hidden, down_w[1])
    kept_ffn_1 = (middle, inverse_ffn, normed_ffn, gate, up)
    act_1 = core_swap(1, width_from_tokens(result.astype(BF)))
    acts = by_layer(act_0, act_1)

    grad_middle, gate_up_1, down_1, gain_ffn_1 = ffn_backward(
        1, top_own, top_branch, down_total, kept_ffn_1, gains[1, 1], gate_up_w[1], down_w[1]
    )
    grad_1, attn_1, gain_attn_1, (acts,) = attn_backward(
        grad_middle, resid_1, inverse_1, kept_attn_1, gains[1, 0], attn_w[1], acts
    )
    grad_1 = grad_1.astype(BF)
    branch = gather_tokens(grad_1)
    grads_1 = core_swap(1, own_width(branch))
    branch, down_total = after(branch, down_grad(branch, hidden_0))
    grad_middle, gate_up_0, down_0, gain_ffn_0 = ffn_backward(
        0, grad_1.astype(F32), branch, down_total, kept_ffn_0, gains[0, 1], gate_up_w[0], down_w[0]
    )
    grad_0, attn_0, gain_attn_0, _ = attn_backward(
        grad_middle, resid_0, inverse_0, kept_attn_0, gains[0, 0], attn_w[0]
    )
    grads_in = by_layer(core_swap(0, width_from_tokens(grad_0.astype(BF))), grads_1)

    def own_layer(first, second):
        return jax.tree.map(by_section, tuple(first), tuple(second))

    def final(zero, one):
        return own_layer(to_core(0, zero), to_core(1, one))

    final_gate, final_up = [
        part[None, :, :units].astype(F32) for part in final(gate_up_0, gate_up_1)
    ]
    final_down = jnp.concatenate(final(down_0, down_1), axis=1)[:, :units].astype(F32).T[None]
    attn_0, final_gate, final_up, final_down = after(attn_0, final_gate, final_up, final_down)
    final_query, final_out = final(attn_0[:, :query_cols], attn_1[:, :query_cols])
    final_keyval = by_section(attn_0[:, query_cols:], attn_1[:, query_cols:]).astype(F32)

    gain_grads_0 = jnp.stack([gain_attn_0, gain_ffn_0])
    gain_grads_1 = jnp.stack([gain_attn_1, gain_ffn_1])
    gain_sums = by_section(gain_grads_0, gain_grads_1) + over_section(
        by_section(gain_grads_1, gain_grads_0)
    )
    gain_parts = [
        lax.dynamic_slice_in_dim(gain_sums, (col ^ k) * width, width, 1) for k in range(cols)
    ]
    gain_sums = gain_parts[0] + sum(over_col(gain_parts[k], k) for k in range(1, cols))
    row_count = lax.axis_size(ROW)
    step = 1
    while step < row_count:
        gain_sums = gain_sums + lax.ppermute(
            gain_sums, ROW, [(i, i ^ step) for i in range(row_count)]
        )
        step *= 2

    return (
        acts.reshape(1, 2, 1, rows, width),
        grads_in.reshape(1, 2, 1, rows, width),
        gain_sums[:1],
        final_query[None].astype(F32),
        final_keyval[None],
        final_out.T[None].astype(F32),
        gain_sums[1:],
        final_gate,
        final_up,
        final_down,
    )


def solution(mesh):
    tokens = P(None, ROW, None, "col")
    gain = P("section", "col")
    rows_cols = P("section", ROW, "col")
    cols_rows = P("section", "col", ROW)
    layers = P("section", None, ROW, None, "col")
    return jax.shard_map(
        step,
        mesh=mesh,
        in_specs=(
            tokens,
            tokens,
            gain,
            rows_cols,
            rows_cols,
            cols_rows,
            gain,
            rows_cols,
            rows_cols,
            cols_rows,
        ),
        out_specs=(
            layers,
            layers,
            gain,
            rows_cols,
            rows_cols,
            cols_rows,
            gain,
            rows_cols,
            rows_cols,
            cols_rows,
        ),
        check_vma=False,
    )
```

```python
import functools
import math

import jax
import jax.numpy as jnp
from jax import lax
from jax.experimental import pallas as pl
from jax.experimental.pallas import tpu as pltpu
from jax.sharding import PartitionSpec as P


HD = 128
SPAN = 4
EPS = 1e-06
THETA = 1000000.0
BF = jnp.bfloat16
F32 = jnp.float32


def dot(left, right, left_dim, right_dim):
    return lax.dot_general(
        left, right, (((left_dim,), (right_dim,)), ((), ())), preferred_element_type=F32
    )


def rope_tables(positions, head_size):
    half = head_size // 2
    freqs = THETA ** (-(jnp.arange(half, dtype=F32) * 2.0) / head_size)
    angles = positions.astype(F32)[:, None] * freqs[None, :]
    angles = jnp.concatenate([angles, angles], axis=-1)
    return (jnp.cos(angles), jnp.sin(angles))


ROW = "row"


def after(value, *others):
    return lax.optimization_barrier((value, *others))


def over_col(block, step):
    count = lax.axis_size("col")
    return lax.ppermute(block, "col", [(i, i ^ step) for i in range(count)])


def over_section(block):
    return lax.ppermute(block, "section", [(0, 1), (1, 0)])


def along_row(block, steps):
    count = lax.axis_size(ROW)
    route = [(i, i + steps) for i in range(count) if 0 <= i % SPAN + steps < SPAN]
    return lax.ppermute(block, ROW, route)


def gather_blocks(own):
    half = own.shape[0] // 2
    first = over_col(own, 1)
    second = over_col(own, 2)
    third_low = over_col(first[:half], 2)
    third_high = over_col(second[half:], 1)
    return own, first, second, jnp.concatenate([third_low, third_high], axis=0)


def gather_tokens(own):
    return jnp.concatenate(gather_blocks(own), axis=0)


def scatter_tokens(partial):
    blocks = jnp.split(partial, 4, axis=0)
    got = [over_col(blocks[k], k).astype(F32) for k in (3, 1, 2)]
    return blocks[0].astype(F32) + got[0] + got[1] + got[2]


def norm(resid, gain):
    inverse = lax.rsqrt(jnp.mean(resid * resid, axis=1, keepdims=True) + EPS)
    return (resid * inverse * gain[None, :]).astype(BF), inverse


def norm_backward(grad_normed, resid, inverse, gain):
    scaled = resid * inverse
    grad_gain = jnp.sum(grad_normed * scaled, axis=0)
    grad_scaled = grad_normed * gain[None, :]
    mean_term = jnp.mean(grad_scaled * scaled, axis=1, keepdims=True)
    return inverse * (grad_scaled - scaled * mean_term), grad_gain


def qkv_kernel(heads, x_ref, w_ref, cos_ref, sign_ref, own_cos_ref, own_sign_ref, q_ref, own_ref):
    raw = jnp.dot(x_ref[...], w_ref[...], preferred_element_type=F32)
    for h in range(heads + 1):
        z = raw[:, h * HD : (h + 1) * HD]
        if h < heads:
            z = z * cos_ref[...] + pltpu.roll(z, HD // 2, 1) * sign_ref[...]
            q_ref[:, h * HD : (h + 1) * HD] = z.astype(BF)
        else:
            z = z * own_cos_ref[...] + pltpu.roll(z, HD // 2, 1) * own_sign_ref[...]
            own_ref[...] = z.astype(BF)


def project_turn(normed, weight, tables, heads):
    rows, depth = normed.shape
    step = rows // 2
    cols = (heads + 1) * HD
    table = pl.BlockSpec((step, HD), lambda i: (i, 0))
    return pl.pallas_call(
        functools.partial(qkv_kernel, heads),
        grid=(2,),
        in_specs=[
            pl.BlockSpec((step, depth), lambda i: (i, 0)),
            pl.BlockSpec((depth, cols), lambda i: (0, 0)),
            *[table] * 4,
        ],
        out_specs=[
            pl.BlockSpec((step, heads * HD), lambda i: (i, 0)),
            pl.BlockSpec((step, HD), lambda i: (i, 0)),
        ],
        out_shape=[
            jax.ShapeDtypeStruct((rows, heads * HD), BF),
            jax.ShapeDtypeStruct((rows, HD), BF),
        ],
        cost_estimate=pl.CostEstimate(
            flops=2 * rows * depth * cols,
            bytes_accessed=2 * (rows * depth + depth * cols + rows * cols),
            transcendentals=0,
        ),
        name="project_turn",
    )(normed, weight, *tables)


def swapped(k, rows):
    quarter = rows // 4
    return [
        (pl.ds(k * rows + i * quarter, quarter), pl.ds((i ^ 1) * quarter, quarter)) for i in range(4)
    ]


def attend_kernel(scale, flag_ref, col_ref, row_ref, q_ref, *refs):
    mine, theirs = refs[:SPAN], refs[SPAN : 2 * SPAN]
    o_ref, lse_ref, k_ref, v_ref, e_ref, total_ref, acc_ref = refs[2 * SPAN :]
    rows = q_ref.shape[0]
    peer, is_key = flag_ref[0], flag_ref[1]
    q = q_ref[...]

    def place(own_ref, other_ref):
        for k in range(SPAN):
            own_ref[k * rows : (k + 1) * rows] = mine[k][...]
            for here, there in swapped(k, rows):
                other_ref[here] = theirs[k][there]

    @pl.when((pl.program_id(0) == 0) & (is_key == 1))
    def _():
        place(k_ref, v_ref)

    @pl.when((pl.program_id(0) == 0) & (is_key == 0))
    def _():
        place(v_ref, k_ref)

    def piece(ref, k):
        return ref[k * rows : (k + 1) * rows]

    def exps(k):
        s = lax.dot_general(
            piece(k_ref, k), q, (((1,), (1,)), ((), ())), preferred_element_type=F32
        )
        return jnp.exp(s * scale)

    e = jnp.where(col_ref[...] <= row_ref[...], exps(0), 0.0)
    e_ref[0] = e
    total_ref[...] = jnp.sum(e, axis=0, keepdims=True)
    for k in range(1, SPAN):

        @pl.when(peer >= k)
        def _():
            e = exps(k)
            e_ref[k] = e
            total_ref[...] += jnp.sum(e, axis=0, keepdims=True)

    total = total_ref[...]
    lse_ref[0] = jnp.log(total)
    shrink = jnp.where(total > 1.0, 2.0**-64, 1.0)
    inverse = 1.0 / (total * shrink)

    def term(k):
        p = ((e_ref[k] * shrink) * inverse).astype(BF)
        return lax.dot_general(
            piece(v_ref, k), p, (((0,), (0,)), ((), ())), preferred_element_type=F32
        )

    acc_ref[...] = term(0)
    for k in range(1, SPAN):

        @pl.when(peer >= k)
        def _():
            acc_ref[...] += term(k)

    o_ref[...] = acc_ref[...].T.astype(BF)


def attend(queries, mine, first, later, flags, order, heads, scale):
    rows = queries.shape[0]
    full = SPAN * rows
    piece = pl.BlockSpec((rows, HD), lambda h: (0, 0))
    whole = pl.BlockSpec((full, HD), lambda h: (0, 0))
    return pl.pallas_call(
        functools.partial(attend_kernel, scale),
        grid=(heads,),
        in_specs=[
            pl.BlockSpec(memory_space=pltpu.SMEM),
            pl.BlockSpec((rows, 1), lambda h: (0, 0)),
            pl.BlockSpec((1, rows), lambda h: (0, 0)),
            pl.BlockSpec((rows, HD), lambda h: (0, h)),
            *[piece] * SPAN,
            piece,
            *[pl.BlockSpec((rows, HD), lambda h, k=k: (k, 0)) for k in range(SPAN - 1)],
        ],
        out_specs=[
            pl.BlockSpec((rows, HD), lambda h: (0, h)),
            pl.BlockSpec((1, 1, rows), lambda h: (h, 0, 0)),
            whole,
            whole,
        ],
        out_shape=[
            jax.ShapeDtypeStruct((rows, heads * HD), BF),
            jax.ShapeDtypeStruct((heads, 1, rows), F32),
            jax.ShapeDtypeStruct((full, HD), BF),
            jax.ShapeDtypeStruct((full, HD), BF),
        ],
        scratch_shapes=[
            pltpu.VMEM((SPAN, rows, rows), F32),
            pltpu.VMEM((1, rows), F32),
            pltpu.VMEM((HD, rows), F32),
        ],
        cost_estimate=pl.CostEstimate(
            flops=4 * heads * rows * full * HD,
            bytes_accessed=4 * rows * HD * (heads + 2 * SPAN),
            transcendentals=heads * rows * full,
        ),
        name="attend",
    )(flags, order[:, None], order[None, :], queries, *mine, first, *[later] * (SPAN - 1))


def attend_back_kernel(
    scale, flag_ref, col_ref, row_ref, cos_ref, sign_ref, q_ref, do_ref, lse_ref, k_ref, v_ref,
    dq_ref, keep_ref, send_ref, p_ref, dp_ref, sum_ref, turn_ref, dk_ref, dv_ref,
):
    h = pl.program_id(0)
    last = pl.num_programs(0) - 1
    rows = q_ref.shape[0]
    peer, is_key = flag_ref[0], flag_ref[1]
    q, do = q_ref[...], do_ref[...]
    lse = lse_ref[0]

    def piece(ref, k):
        return ref[k * rows : (k + 1) * rows]

    def first(k):
        nt = (((1,), (1,)), ((), ()))
        s = lax.dot_general(piece(k_ref, k), q, nt, preferred_element_type=F32)
        p = jnp.exp(s * scale - lse)
        if k == 0:
            p = jnp.where(col_ref[...] <= row_ref[...], p, 0.0)
        dp = lax.dot_general(piece(v_ref, k), do, nt, preferred_element_type=F32)
        p_ref[k] = p
        dp_ref[k] = dp
        return jnp.sum(p * dp, axis=0, keepdims=True)

    def second(k):
        p = p_ref[k]
        ds = (p * (dp_ref[k] - sum_ref[...])).astype(BF)
        dk = jnp.dot(ds, q, preferred_element_type=F32)
        dv = jnp.dot(p.astype(BF), do, preferred_element_type=F32)

        @pl.when(h == 0)
        def _():
            dk_ref[k * rows : (k + 1) * rows] = dk
            dv_ref[k * rows : (k + 1) * rows] = dv

        @pl.when(h > 0)
        def _():
            dk_ref[k * rows : (k + 1) * rows] += dk
            dv_ref[k * rows : (k + 1) * rows] += dv

        return lax.dot_general(
            piece(k_ref, k), ds, (((0,), (0,)), ((), ())), preferred_element_type=F32
        )

    sum_ref[...] = first(0)
    for k in range(1, SPAN):

        @pl.when(peer >= k)
        def _():
            sum_ref[...] += first(k)

    turn_ref[...] = second(0)
    for k in range(1, SPAN):

        @pl.when(peer >= k)
        def _():
            turn_ref[...] += second(k)

        @pl.when((peer < k) & (h == 0))
        def _():
            dk_ref[k * rows : (k + 1) * rows] = jnp.zeros((rows, HD), F32)
            dv_ref[k * rows : (k + 1) * rows] = jnp.zeros((rows, HD), F32)

    dq = turn_ref[...].T * scale
    dq = dq * cos_ref[...] - pltpu.roll(dq, HD // 2, 1) * sign_ref[...]
    dq_ref[...] = dq.astype(BF)

    @pl.when((h == last) & (is_key == 1))
    def _():
        keep_ref[...] = dk_ref[...] * scale
        for k in range(SPAN):
            for here, there in swapped(k, rows):
                to = pl.ds(k * rows + there.start, there.size)
                send_ref[to] = dv_ref[here].astype(BF)

    @pl.when((h == last) & (is_key == 0))
    def _():
        keep_ref[...] = dv_ref[...]
        for k in range(SPAN):
            for here, there in swapped(k, rows):
                to = pl.ds(k * rows + there.start, there.size)
                send_ref[to] = (dk_ref[here] * scale).astype(BF)


def attend_back(queries, grads, lse, keys, values, flags, order, cosine, signed, heads, scale):
    rows = queries.shape[0]
    full = SPAN * rows
    whole = pl.BlockSpec((full, HD), lambda h: (0, 0))
    table = pl.BlockSpec((rows, HD), lambda h: (0, 0))
    one_head = pl.BlockSpec((rows, HD), lambda h: (0, h))
    return pl.pallas_call(
        functools.partial(attend_back_kernel, scale),
        grid=(heads,),
        in_specs=[
            pl.BlockSpec(memory_space=pltpu.SMEM),
            pl.BlockSpec((rows, 1), lambda h: (0, 0)),
            pl.BlockSpec((1, rows), lambda h: (0, 0)),
            table,
            table,
            one_head,
            one_head,
            pl.BlockSpec((1, 1, rows), lambda h: (h, 0, 0)),
            whole,
            whole,
        ],
        out_specs=[one_head, whole, whole],
        out_shape=[
            jax.ShapeDtypeStruct((rows, heads * HD), BF),
            jax.ShapeDtypeStruct((full, HD), F32),
            jax.ShapeDtypeStruct((full, HD), BF),
        ],
        scratch_shapes=[
            pltpu.VMEM((SPAN, rows, rows), F32),
            pltpu.VMEM((SPAN, rows, rows), F32),
            pltpu.VMEM((1, rows), F32),
            pltpu.VMEM((HD, rows), F32),
            pltpu.VMEM((full, HD), F32),
            pltpu.VMEM((full, HD), F32),
        ],
        cost_estimate=pl.CostEstimate(
            flops=10 * heads * rows * full * HD,
            bytes_accessed=4 * rows * HD * (2 * heads + 2 * SPAN),
            transcendentals=heads * rows * full,
        ),
        name="attend_back",
    )(flags, order[:, None], order[None, :], cosine, signed, queries, grads, lse, keys, values)


def settle_kernel(flag_ref, *refs):
    half, out_ref = len(refs) // 2, refs[-1]
    blocks = (refs[:half], refs[half:-1])
    for layer, parts in enumerate(blocks):
        for i, part in enumerate(parts):
            mine = flag_ref[0] == layer
            if len(parts) > 1:
                low = pl.program_id(0) < pl.num_programs(0) // 2
                mine = mine & (low if i == 0 else jnp.logical_not(low))

            @pl.when(mine)
            def _():
                out_ref[...] = part[...].astype(F32).T


def settle(flag, zero, one, units):
    shard = zero[0].shape[0]
    tile = 128
    count = zero[0].shape[1] // tile
    if len(zero) == 1:
        maps = [lambda j: (0, j)]
    else:
        maps = [
            lambda j: (0, jnp.minimum(j, count - 1)),
            lambda j: (0, jnp.maximum(j - count, 0)),
        ]
    specs = [pl.BlockSpec((shard, tile), index_map) for index_map in maps]
    return pl.pallas_call(
        settle_kernel,
        grid=(count * len(zero),),
        in_specs=[pl.BlockSpec(memory_space=pltpu.SMEM), *specs, *specs],
        out_specs=pl.BlockSpec((tile, shard), lambda j: (j, 0)),
        out_shape=jax.ShapeDtypeStruct((units, shard), F32),
        cost_estimate=pl.CostEstimate(
            flops=units * shard, bytes_accessed=8 * units * shard, transcendentals=0
        ),
        name="settle",
    )(flag, *zero, *one)


def step(layer_input, g_out, attn_gain, w_query, w_keyval, w_out, ffn_gain, w_gate, w_up, w_down):
    section = lax.axis_index("section")
    col = lax.axis_index("col")
    peer = lax.axis_index(ROW) % SPAN
    cols = lax.axis_size("col")
    is_first = section == 0
    is_key = col % 2 == 0
    rows = layer_input.shape[2]
    width = layer_input.shape[3]
    own_rows = rows // cols
    full = width * cols
    heads = w_query.shape[2] // HD
    query_cols = w_query.shape[2]
    qkv_cols = query_cols + HD
    units = w_gate.shape[2]
    scale = 1.0 / math.sqrt(HD)

    def by_section(first, second):
        return jnp.where(is_first, first, second)

    def by_key(first, second):
        return jnp.where(is_key, first, second)

    def xor_rows(block):
        return jnp.concatenate(
            [lax.dynamic_slice_in_dim(block, (col ^ k) * own_rows, own_rows, 0) for k in range(cols)],
            axis=0,
        )

    def reorder(block, k):
        parts = jnp.split(block, cols, axis=0)
        return jnp.concatenate([parts[m ^ k] for m in range(cols)], axis=0)

    def gather_width(block):
        parts = [reorder(part, k) for k, part in enumerate(gather_blocks(xor_rows(block)))]
        total = jnp.zeros((block.shape[0], full), block.dtype)
        for k, part in enumerate(parts):
            total = lax.dynamic_update_slice_in_dim(total, part, (col ^ k) * width, 1)
        return total

    def tokens_from_width(block):
        total = jnp.zeros((own_rows, full), block.dtype)
        for k in range(cols):
            part = lax.dynamic_slice_in_dim(block, (col ^ k) * own_rows, own_rows, 0)
            if k:
                part = over_col(part, k)
            total = lax.dynamic_update_slice_in_dim(total, part, (col ^ k) * width, 1)
        return total

    def width_from_tokens(block):
        total = jnp.zeros((rows, width), block.dtype)
        for k in range(cols):
            part = lax.dynamic_slice_in_dim(block, (col ^ k) * width, width, 1)
            if k:
                part = over_col(part, k)
            total = lax.dynamic_update_slice_in_dim(total, part, (col ^ k) * own_rows, 0)
        return total

    gains_own = jnp.stack([attn_gain[0], ffn_gain[0]])
    gains_other = over_section(gains_own)
    gains_part = jnp.stack([by_section(gains_own, gains_other), by_section(gains_other, gains_own)])
    gains = jnp.zeros((2, 2, full), F32)
    for k in range(cols):
        part = over_col(gains_part, k) if k else gains_part
        gains = lax.dynamic_update_slice_in_dim(gains, part, (col ^ k) * width, 2)

    shard = w_query.shape[1]
    attn_own = jnp.concatenate([w_query[0], w_keyval[0], w_out[0].T], axis=1)
    half_rows = shard // 2
    wide = -(-units // 256) * 256
    half_units = wide // 2

    def both_layers(low, high):
        got = over_section(by_section(high, low))
        return by_section(low, got), by_section(got, high)

    def widen(array):
        return jnp.pad(array, ((0, 0), (0, wide - units)))

    down_own = widen(w_down[0].T)
    attn_parts = both_layers(attn_own[:half_rows], attn_own[half_rows:])
    gate_up_parts = both_layers(widen(w_gate[0]), widen(w_up[0]))
    down_parts = both_layers(down_own[:, :half_units], down_own[:, half_units:])

    def gather_layers(part):
        return lax.all_gather(part, ("section", ROW), axis=0, tiled=True)

    def split_layers(both):
        return both[:full], both[full:]

    def gather_attn(part):
        return lax.all_gather(part, (ROW, "section"), axis=0, tiled=True)

    order = jnp.concatenate(
        [(col ^ k) * own_rows + jnp.arange(own_rows, dtype=jnp.int32) for k in range(cols)]
    )
    positions = peer * rows + order
    cosine, sine = rope_tables(positions, HD)
    signed = jnp.where(jnp.arange(HD) < HD // 2, -sine, sine)

    def swap_halves(values):
        return jnp.concatenate([values[:, HD // 2 :], values[:, : HD // 2]], axis=1)

    flags = jnp.stack([peer, jnp.where(is_key, 1, 0)]).astype(jnp.int32)
    own_cosine = by_key(cosine, jnp.ones_like(cosine))
    own_signed = by_key(signed, jnp.zeros_like(signed))
    tables = (cosine, signed, own_cosine, own_signed)

    def attn_forward(normed, attn_w):
        queries, own = project_turn(normed, attn_w, tables, heads)
        first = over_col(own, 1)
        mine = [own] + [along_row(own, k) for k in range(1, SPAN)]
        later = over_col(jnp.concatenate(mine[1:], axis=0), 1)
        attended, lse, keys, values = attend(
            queries, mine, first, later, flags, order, heads, scale
        )
        return attended, (normed, queries, keys, values, lse, attended)

    def attn_out(resid, attended, attn_w):
        return resid + scatter_tokens(dot(attended, attn_w[:, qkv_cols:], 1, 1).astype(BF))

    def ffn_gather(middle, ffn_gain):
        normed_own, inverse_ffn = norm(middle, ffn_gain)
        return gather_tokens(normed_own), inverse_ffn

    def ffn_in(normed_ffn, gate_up_w):
        gate_up_w = split_layers(gate_up_w)
        gate = dot(normed_ffn, gate_up_w[0], 1, 0)
        up = dot(normed_ffn, gate_up_w[1], 1, 0)
        return gate.astype(BF), up.astype(BF), (jax.nn.silu(gate) * up).astype(BF)

    def ffn_out(hidden, down_w):
        down_w = split_layers(down_w)
        out = dot(hidden[:, :half_units], down_w[0], 1, 1)
        return scatter_tokens((out + dot(hidden[:, half_units:], down_w[1], 1, 1)).astype(BF))

    def swap_add(left, first, second):
        got = over_section(dot(left, by_section(second, first), 0, 0).astype(BF))
        return (dot(left, by_section(first, second), 0, 0) + got.astype(F32)).astype(BF)

    def scatter_rows(total):
        return lax.psum_scatter(total, ROW, scatter_dimension=0, tiled=True)

    def down_grad(grad_branch, hidden):
        return swap_add(grad_branch, hidden[:, :half_units], hidden[:, half_units:])

    def ffn_backward(layer, grad_own, grad_branch, down_total, kept, ffn_gain, gate_up_w, down_w):
        middle, inverse_ffn, normed_ffn, gate, up = kept
        gate_up_w, down_w = split_layers(gate_up_w), split_layers(down_w)
        down_sum = scatter_rows(down_total)
        grad_hidden = jnp.concatenate(
            [dot(grad_branch, down_w[0], 1, 0), dot(grad_branch, down_w[1], 1, 0)], axis=1
        )
        gate, up = gate.astype(F32), up.astype(F32)
        sigma = jax.nn.sigmoid(gate)
        dgate = (grad_hidden * up * sigma * (1.0 + gate * (1.0 - sigma))).astype(BF)
        dup = (grad_hidden * gate * sigma).astype(BF)
        gate_up_total = swap_add(normed_ffn, dgate, dup)
        if layer == 0:
            dgate, dup, gate_up_total = after(dgate, dup, gate_up_total)
        grad_normed_ffn = (dot(dgate, gate_up_w[0], 1, 1) + dot(dup, gate_up_w[1], 1, 1)).astype(BF)
        grad_normed_ffn = scatter_tokens(grad_normed_ffn)
        if layer == 1:
            grad_normed_ffn, gate_up_total = after(grad_normed_ffn, gate_up_total)
        gate_up_sum = scatter_rows(gate_up_total)
        grad_middle, grad_gain_ffn = norm_backward(grad_normed_ffn, middle, inverse_ffn, ffn_gain)
        grad_middle = grad_own + grad_middle
        return grad_middle, gate_up_sum, down_sum, grad_gain_ffn

    def attn_backward(grad_middle, resid, inverse_attn, kept, attn_gain, attn_w, *others):
        normed, queries, keys, values, lse, attended = kept
        w_qkv, w_o = attn_w[:, :qkv_cols], attn_w[:, qkv_cols:]
        grad_attn_out = gather_tokens(grad_middle.astype(BF))
        grad_attended = dot(grad_attn_out, w_o, 1, 0).astype(BF)
        grad_query_raw, grad_keep, grad_send = attend_back(
            queries, grad_attended, lse, keys, values, flags, order, cosine, signed, heads, scale
        )
        grad_keep = grad_keep + over_col(grad_send, 1).astype(F32)
        pieces = jnp.split(grad_keep, SPAN, axis=0)
        grad_mine = pieces[0]
        for k in range(1, SPAN):
            grad_mine = grad_mine + along_row(pieces[k].astype(BF), -k).astype(F32)
        grad_wout = dot(grad_attn_out, attended, 0, 0).astype(BF)
        grad_wquery = dot(normed, grad_query_raw, 0, 0).astype(BF)
        got = over_section(by_section(grad_wout, grad_wquery))
        early = by_section(grad_wquery, grad_wout).astype(F32) + got.astype(F32)
        grad_mine, early, *others = after(grad_mine, early.astype(BF), *others)
        grad_keyval = grad_mine * own_cosine - swap_halves(grad_mine) * own_signed
        grad_keyval = grad_keyval.astype(BF)
        late = dot(normed, grad_keyval, 0, 0).astype(BF)
        late = late.astype(F32) + over_section(late).astype(F32)
        total = jnp.concatenate([early, late.astype(BF)], axis=1)
        grad_normed = (
            dot(grad_query_raw, w_qkv[:, :query_cols], 1, 1)
            + dot(grad_keyval, w_qkv[:, query_cols:], 1, 1)
        ).astype(BF)
        grad_normed, total = after(scatter_tokens(grad_normed), total)
        attn_sum = scatter_rows(total)
        grad_resid, grad_gain_attn = norm_backward(grad_normed, resid, inverse_attn, attn_gain)
        grad_resid = grad_middle + grad_resid
        return grad_resid, attn_sum, grad_gain_attn, others

    def own_width(block):
        block = lax.dynamic_slice_in_dim(block, col * width, width, 1)
        return xor_rows(block)

    def core_swap(layer, block):
        return block, lax.ppermute(block, "section", [(1 - layer, layer)])

    def by_layer(first, second):
        first, first_got = first
        second, second_got = second
        return jnp.stack([by_section(first, second_got), by_section(first_got, second)])

    def to_core(layer, block):
        got = lax.ppermute(block, "section", [(1 - layer, layer)])
        return (block, got) if layer == 0 else (got, block)

    attn_w = [gather_attn(attn_parts[0])]
    x_full = gather_width(lax.dynamic_index_in_dim(layer_input[:, 0], section, 0, keepdims=False))
    ffn_w = gather_layers(jnp.concatenate([gate_up_parts[0], down_parts[0]], axis=1))
    gate_up_w, down_w = [ffn_w[:, :wide]], [ffn_w[:, wide:]]
    normed, inverse = norm(x_full.astype(F32), gains[0, 0])
    resid_0, inverse_0 = x_full[:own_rows].astype(F32), inverse[:own_rows]
    attended, kept_attn_0 = attn_forward(normed, attn_w[0])
    _, attn_part = after(attended, attn_parts[1])
    attn_w.append(gather_attn(attn_part))
    middle = attn_out(resid_0, attended, attn_w[0])
    _, gate_up_part = after(middle, gate_up_parts[1])
    gate_up_w.append(gather_layers(gate_up_part))
    normed_ffn, inverse_ffn = ffn_gather(middle, gains[0, 1])
    gate, up, hidden = ffn_in(normed_ffn, gate_up_w[0])
    _, down_part = after(hidden, down_parts[1])
    down_w.append(gather_layers(down_part))
    result = middle + ffn_out(hidden, down_w[0])
    kept_ffn_0 = (middle, inverse_ffn, normed_ffn, gate, up)
    hidden_0 = hidden
    x_full = gather_tokens(result.astype(BF))
    act_0 = core_swap(0, own_width(x_full))
    normed, inverse = norm(x_full.astype(F32), gains[1, 0])
    resid_1, inverse_1 = x_full[:own_rows].astype(F32), inverse[:own_rows]
    attended, kept_attn_1 = attn_forward(normed, attn_w[1])
    _, g_out = after(attended, g_out)
    middle = attn_out(resid_1, attended, attn_w[1])
    normed_ffn, inverse_ffn = ffn_gather(middle, gains[1, 1])
    top = lax.dynamic_index_in_dim(g_out[:, 0], section, 0, keepdims=False)
    top_branch = gather_width(top.astype(BF))
    top_own = tokens_from_width(top)
    gate, up, hidden = ffn_in(normed_ffn, gate_up_w[1])
    down_w[1], down_total, top_own = after(down_w[1], down_grad(top_branch, hidden), top_own)
    result = middle + ffn_out(hidden, down_w[1])
    kept_ffn_1 = (middle, inverse_ffn, normed_ffn, gate, up)
    act_1 = core_swap(1, width_from_tokens(result.astype(BF)))
    acts = by_layer(act_0, act_1)

    grad_middle, gate_up_1, down_1, gain_ffn_1 = ffn_backward(
        1, top_own, top_branch, down_total, kept_ffn_1, gains[1, 1], gate_up_w[1], down_w[1]
    )
    grad_1, attn_1, gain_attn_1, (acts,) = attn_backward(
        grad_middle, resid_1, inverse_1, kept_attn_1, gains[1, 0], attn_w[1], acts
    )
    grad_1 = grad_1.astype(BF)
    branch = gather_tokens(grad_1)
    grads_1 = core_swap(1, own_width(branch))
    branch, down_total = after(branch, down_grad(branch, hidden_0))
    grad_middle, gate_up_0, down_0, gain_ffn_0 = ffn_backward(
        0, grad_1.astype(F32), branch, down_total, kept_ffn_0, gains[0, 1], gate_up_w[0], down_w[0]
    )
    grad_0, attn_0, gain_attn_0, _ = attn_backward(
        grad_middle, resid_0, inverse_0, kept_attn_0, gains[0, 0], attn_w[0]
    )
    grads_in = by_layer(core_swap(0, width_from_tokens(grad_0.astype(BF))), grads_1)

    def own_layer(first, second):
        return jax.tree.map(by_section, tuple(first), tuple(second))

    def final(zero, one):
        return own_layer(to_core(0, zero), to_core(1, one))

    flag = jnp.reshape(section, (1,)).astype(jnp.int32)
    gate_up_0, gate_up_1 = to_core(0, gate_up_0), to_core(1, gate_up_1)
    final_gate = settle(flag, gate_up_0[:1], gate_up_1[:1], units)
    final_up = settle(flag, gate_up_0[1:], gate_up_1[1:], units)
    final_down = settle(flag, to_core(0, down_0), to_core(1, down_1), units)
    attn_0, final_gate, final_up, final_down = after(attn_0, final_gate, final_up, final_down)
    final_query, final_out = final(attn_0[:, :query_cols], attn_1[:, :query_cols])
    final_keyval = by_section(attn_0[:, query_cols:], attn_1[:, query_cols:]).astype(F32)

    gain_grads_0 = jnp.stack([gain_attn_0, gain_ffn_0])
    gain_grads_1 = jnp.stack([gain_attn_1, gain_ffn_1])
    gain_sums = by_section(gain_grads_0, gain_grads_1) + over_section(
        by_section(gain_grads_1, gain_grads_0)
    )
    gain_parts = [
        lax.dynamic_slice_in_dim(gain_sums, (col ^ k) * width, width, 1) for k in range(cols)
    ]
    gain_sums = gain_parts[0] + sum(over_col(gain_parts[k], k) for k in range(1, cols))
    row_count = lax.axis_size(ROW)
    step = 1
    while step < row_count:
        gain_sums = gain_sums + lax.ppermute(
            gain_sums, ROW, [(i, i ^ step) for i in range(row_count)]
        )
        step *= 2

    return (
        acts.reshape(1, 2, 1, rows, width),
        grads_in.reshape(1, 2, 1, rows, width),
        gain_sums[:1],
        final_query[None].astype(F32),
        final_keyval[None],
        final_out.T[None].astype(F32),
        gain_sums[1:],
        final_gate.T[None],
        final_up.T[None],
        final_down[None],
    )


def solution(mesh):
    tokens = P(None, ROW, None, "col")
    gain = P("section", "col")
    rows_cols = P("section", ROW, "col")
    cols_rows = P("section", "col", ROW)
    layers = P("section", None, ROW, None, "col")
    return jax.shard_map(
        step,
        mesh=mesh,
        in_specs=(
            tokens,
            tokens,
            gain,
            rows_cols,
            rows_cols,
            cols_rows,
            gain,
            rows_cols,
            rows_cols,
            cols_rows,
        ),
        out_specs=(
            layers,
            layers,
            gain,
            rows_cols,
            rows_cols,
            cols_rows,
            gain,
            rows_cols,
            rows_cols,
            cols_rows,
        ),
        check_vma=False,
    )
```

```python
import functools
import math

import jax
import jax.numpy as jnp
from jax import lax
from jax.experimental import pallas as pl
from jax.experimental.pallas import tpu as pltpu
from jax.sharding import PartitionSpec as P


HD = 128
SPAN = 4
EPS = 1e-06
THETA = 1000000.0
BF = jnp.bfloat16
F32 = jnp.float32


def dot(left, right, left_dim, right_dim):
    return lax.dot_general(
        left, right, (((left_dim,), (right_dim,)), ((), ())), preferred_element_type=F32
    )


def rope_tables(positions, head_size):
    half = head_size // 2
    freqs = THETA ** (-(jnp.arange(half, dtype=F32) * 2.0) / head_size)
    angles = positions.astype(F32)[:, None] * freqs[None, :]
    angles = jnp.concatenate([angles, angles], axis=-1)
    return (jnp.cos(angles), jnp.sin(angles))


ROW = "row"


def after(value, *others):
    return lax.optimization_barrier((value, *others))


def over_col(block, step):
    count = lax.axis_size("col")
    return lax.ppermute(block, "col", [(i, i ^ step) for i in range(count)])


def over_section(block):
    return lax.ppermute(block, "section", [(0, 1), (1, 0)])


def along_row(block, steps):
    count = lax.axis_size(ROW)
    route = [(i, i + steps) for i in range(count) if 0 <= i % SPAN + steps < SPAN]
    return lax.ppermute(block, ROW, route)


def gather_blocks(own):
    half = own.shape[0] // 2
    first = over_col(own, 1)
    second = over_col(own, 2)
    third_low = over_col(first[:half], 2)
    third_high = over_col(second[half:], 1)
    return own, first, second, jnp.concatenate([third_low, third_high], axis=0)


def gather_tokens(own):
    return jnp.concatenate(gather_blocks(own), axis=0)


def scatter_tokens(partial):
    blocks = jnp.split(partial, 4, axis=0)
    got = [over_col(blocks[k], k).astype(F32) for k in (3, 1, 2)]
    return blocks[0].astype(F32) + got[0] + got[1] + got[2]


def norm(resid, gain):
    inverse = lax.rsqrt(jnp.mean(resid * resid, axis=1, keepdims=True) + EPS)
    return (resid * inverse * gain[None, :]).astype(BF), inverse


def norm_backward(grad_normed, resid, inverse, gain):
    scaled = resid * inverse
    grad_gain = jnp.sum(grad_normed * scaled, axis=0)
    grad_scaled = grad_normed * gain[None, :]
    mean_term = jnp.mean(grad_scaled * scaled, axis=1, keepdims=True)
    return inverse * (grad_scaled - scaled * mean_term), grad_gain


def qkv_kernel(heads, x_ref, w_ref, cos_ref, sign_ref, own_cos_ref, own_sign_ref, q_ref, own_ref):
    raw = jnp.dot(x_ref[...], w_ref[...], preferred_element_type=F32)
    for h in range(heads + 1):
        z = raw[:, h * HD : (h + 1) * HD]
        if h < heads:
            z = z * cos_ref[...] + pltpu.roll(z, HD // 2, 1) * sign_ref[...]
            q_ref[:, h * HD : (h + 1) * HD] = z.astype(BF)
        else:
            z = z * own_cos_ref[...] + pltpu.roll(z, HD // 2, 1) * own_sign_ref[...]
            own_ref[...] = z.astype(BF)


def project_turn(normed, weight, layer, tables, heads):
    rows, depth = normed.shape
    step = rows // 2
    cols = (heads + 1) * HD
    table = pl.BlockSpec((step, HD), lambda i: (i, 0))
    return pl.pallas_call(
        functools.partial(qkv_kernel, heads),
        grid=(2,),
        in_specs=[
            pl.BlockSpec((step, depth), lambda i: (i, 0)),
            pl.BlockSpec((depth, cols), lambda i: (0, layer)),
            *[table] * 4,
        ],
        out_specs=[
            pl.BlockSpec((step, heads * HD), lambda i: (i, 0)),
            pl.BlockSpec((step, HD), lambda i: (i, 0)),
        ],
        out_shape=[
            jax.ShapeDtypeStruct((rows, heads * HD), BF),
            jax.ShapeDtypeStruct((rows, HD), BF),
        ],
        cost_estimate=pl.CostEstimate(
            flops=2 * rows * depth * cols,
            bytes_accessed=2 * (rows * depth + depth * cols + rows * cols),
            transcendentals=0,
        ),
        name="project_turn",
    )(normed, weight, *tables)


def swapped(k, rows):
    quarter = rows // 4
    return [
        (pl.ds(k * rows + i * quarter, quarter), pl.ds((i ^ 1) * quarter, quarter)) for i in range(4)
    ]


def attend_kernel(scale, flag_ref, col_ref, row_ref, q_ref, *refs):
    mine, theirs = refs[:SPAN], refs[SPAN : 2 * SPAN]
    o_ref, lse_ref, k_ref, v_ref, e_ref, total_ref, acc_ref = refs[2 * SPAN :]
    rows = q_ref.shape[0]
    peer, is_key = flag_ref[0], flag_ref[1]
    q = q_ref[...]

    def place(own_ref, other_ref):
        for k in range(SPAN):
            own_ref[k * rows : (k + 1) * rows] = mine[k][...]
            for here, there in swapped(k, rows):
                other_ref[here] = theirs[k][there]

    @pl.when((pl.program_id(0) == 0) & (is_key == 1))
    def _():
        place(k_ref, v_ref)

    @pl.when((pl.program_id(0) == 0) & (is_key == 0))
    def _():
        place(v_ref, k_ref)

    def piece(ref, k):
        return ref[k * rows : (k + 1) * rows]

    def exps(k):
        s = lax.dot_general(
            piece(k_ref, k), q, (((1,), (1,)), ((), ())), preferred_element_type=F32
        )
        return jnp.exp(s * scale)

    e = jnp.where(col_ref[...] <= row_ref[...], exps(0), 0.0)
    e_ref[0] = e
    total_ref[...] = jnp.sum(e, axis=0, keepdims=True)
    for k in range(1, SPAN):

        @pl.when(peer >= k)
        def _():
            e = exps(k)
            e_ref[k] = e
            total_ref[...] += jnp.sum(e, axis=0, keepdims=True)

    total = total_ref[...]
    lse_ref[0] = jnp.log(total)
    shrink = jnp.where(total > 1.0, 2.0**-64, 1.0)
    inverse = 1.0 / (total * shrink)

    def term(k):
        p = ((e_ref[k] * shrink) * inverse).astype(BF)
        return lax.dot_general(
            piece(v_ref, k), p, (((0,), (0,)), ((), ())), preferred_element_type=F32
        )

    acc_ref[...] = term(0)
    for k in range(1, SPAN):

        @pl.when(peer >= k)
        def _():
            acc_ref[...] += term(k)

    o_ref[...] = acc_ref[...].T.astype(BF)


def attend(queries, mine, first, later, flags, order, heads, scale):
    rows = queries.shape[0]
    full = SPAN * rows
    piece = pl.BlockSpec((rows, HD), lambda h: (0, 0))
    whole = pl.BlockSpec((full, HD), lambda h: (0, 0))
    return pl.pallas_call(
        functools.partial(attend_kernel, scale),
        grid=(heads,),
        in_specs=[
            pl.BlockSpec(memory_space=pltpu.SMEM),
            pl.BlockSpec((rows, 1), lambda h: (0, 0)),
            pl.BlockSpec((1, rows), lambda h: (0, 0)),
            pl.BlockSpec((rows, HD), lambda h: (0, h)),
            *[piece] * SPAN,
            piece,
            *[pl.BlockSpec((rows, HD), lambda h, k=k: (k, 0)) for k in range(SPAN - 1)],
        ],
        out_specs=[
            pl.BlockSpec((rows, HD), lambda h: (0, h)),
            pl.BlockSpec((1, 1, rows), lambda h: (h, 0, 0)),
            whole,
            whole,
        ],
        out_shape=[
            jax.ShapeDtypeStruct((rows, heads * HD), BF),
            jax.ShapeDtypeStruct((heads, 1, rows), F32),
            jax.ShapeDtypeStruct((full, HD), BF),
            jax.ShapeDtypeStruct((full, HD), BF),
        ],
        scratch_shapes=[
            pltpu.VMEM((SPAN, rows, rows), F32),
            pltpu.VMEM((1, rows), F32),
            pltpu.VMEM((HD, rows), F32),
        ],
        cost_estimate=pl.CostEstimate(
            flops=4 * heads * rows * full * HD,
            bytes_accessed=4 * rows * HD * (heads + 2 * SPAN),
            transcendentals=heads * rows * full,
        ),
        name="attend",
    )(flags, order[:, None], order[None, :], queries, *mine, first, *[later] * (SPAN - 1))


def attend_back_kernel(
    scale, flag_ref, col_ref, row_ref, cos_ref, sign_ref, q_ref, do_ref, lse_ref, k_ref, v_ref,
    dq_ref, keep_ref, send_ref, p_ref, dp_ref, sum_ref, turn_ref, dk_ref, dv_ref,
):
    h = pl.program_id(0)
    last = pl.num_programs(0) - 1
    rows = q_ref.shape[0]
    peer, is_key = flag_ref[0], flag_ref[1]
    q, do = q_ref[...], do_ref[...]
    lse = lse_ref[0]

    def piece(ref, k):
        return ref[k * rows : (k + 1) * rows]

    def first(k):
        nt = (((1,), (1,)), ((), ()))
        s = lax.dot_general(piece(k_ref, k), q, nt, preferred_element_type=F32)
        p = jnp.exp(s * scale - lse)
        if k == 0:
            p = jnp.where(col_ref[...] <= row_ref[...], p, 0.0)
        dp = lax.dot_general(piece(v_ref, k), do, nt, preferred_element_type=F32)
        p_ref[k] = p
        dp_ref[k] = dp
        return jnp.sum(p * dp, axis=0, keepdims=True)

    def second(k):
        p = p_ref[k]
        ds = (p * (dp_ref[k] - sum_ref[...])).astype(BF)
        dk = jnp.dot(ds, q, preferred_element_type=F32)
        dv = jnp.dot(p.astype(BF), do, preferred_element_type=F32)

        @pl.when(h == 0)
        def _():
            dk_ref[k * rows : (k + 1) * rows] = dk
            dv_ref[k * rows : (k + 1) * rows] = dv

        @pl.when(h > 0)
        def _():
            dk_ref[k * rows : (k + 1) * rows] += dk
            dv_ref[k * rows : (k + 1) * rows] += dv

        return lax.dot_general(
            piece(k_ref, k), ds, (((0,), (0,)), ((), ())), preferred_element_type=F32
        )

    sum_ref[...] = first(0)
    for k in range(1, SPAN):

        @pl.when(peer >= k)
        def _():
            sum_ref[...] += first(k)

    turn_ref[...] = second(0)
    for k in range(1, SPAN):

        @pl.when(peer >= k)
        def _():
            turn_ref[...] += second(k)

        @pl.when((peer < k) & (h == 0))
        def _():
            dk_ref[k * rows : (k + 1) * rows] = jnp.zeros((rows, HD), F32)
            dv_ref[k * rows : (k + 1) * rows] = jnp.zeros((rows, HD), F32)

    dq = turn_ref[...].T * scale
    dq = dq * cos_ref[...] - pltpu.roll(dq, HD // 2, 1) * sign_ref[...]
    dq_ref[...] = dq.astype(BF)

    @pl.when((h == last) & (is_key == 1))
    def _():
        keep_ref[...] = dk_ref[...] * scale
        for k in range(SPAN):
            for here, there in swapped(k, rows):
                to = pl.ds(k * rows + there.start, there.size)
                send_ref[to] = dv_ref[here].astype(BF)

    @pl.when((h == last) & (is_key == 0))
    def _():
        keep_ref[...] = dv_ref[...]
        for k in range(SPAN):
            for here, there in swapped(k, rows):
                to = pl.ds(k * rows + there.start, there.size)
                send_ref[to] = (dk_ref[here] * scale).astype(BF)


def attend_back(queries, grads, lse, keys, values, flags, order, cosine, signed, heads, scale):
    rows = queries.shape[0]
    full = SPAN * rows
    whole = pl.BlockSpec((full, HD), lambda h: (0, 0))
    table = pl.BlockSpec((rows, HD), lambda h: (0, 0))
    one_head = pl.BlockSpec((rows, HD), lambda h: (0, h))
    return pl.pallas_call(
        functools.partial(attend_back_kernel, scale),
        grid=(heads,),
        in_specs=[
            pl.BlockSpec(memory_space=pltpu.SMEM),
            pl.BlockSpec((rows, 1), lambda h: (0, 0)),
            pl.BlockSpec((1, rows), lambda h: (0, 0)),
            table,
            table,
            one_head,
            one_head,
            pl.BlockSpec((1, 1, rows), lambda h: (h, 0, 0)),
            whole,
            whole,
        ],
        out_specs=[one_head, whole, whole],
        out_shape=[
            jax.ShapeDtypeStruct((rows, heads * HD), BF),
            jax.ShapeDtypeStruct((full, HD), F32),
            jax.ShapeDtypeStruct((full, HD), BF),
        ],
        scratch_shapes=[
            pltpu.VMEM((SPAN, rows, rows), F32),
            pltpu.VMEM((SPAN, rows, rows), F32),
            pltpu.VMEM((1, rows), F32),
            pltpu.VMEM((HD, rows), F32),
            pltpu.VMEM((full, HD), F32),
            pltpu.VMEM((full, HD), F32),
        ],
        cost_estimate=pl.CostEstimate(
            flops=10 * heads * rows * full * HD,
            bytes_accessed=4 * rows * HD * (2 * heads + 2 * SPAN),
            transcendentals=heads * rows * full,
        ),
        name="attend_back",
    )(flags, order[:, None], order[None, :], cosine, signed, queries, grads, lse, keys, values)


def settle_kernel(flag_ref, *refs):
    half, out_ref = len(refs) // 2, refs[-1]
    blocks = (refs[:half], refs[half:-1])
    for layer, parts in enumerate(blocks):
        for i, part in enumerate(parts):
            mine = flag_ref[0] == layer
            if len(parts) > 1:
                low = pl.program_id(0) < pl.num_programs(0) // 2
                mine = mine & (low if i == 0 else jnp.logical_not(low))

            @pl.when(mine)
            def _():
                out_ref[...] = part[...].astype(F32).T


def settle(flag, zero, one, units):
    shard = zero[0].shape[0]
    tile = zero[0].shape[1] // 3
    count = 3
    if len(zero) == 1:
        maps = [lambda j: (0, j)]
    else:
        maps = [
            lambda j: (0, jnp.minimum(j, count - 1)),
            lambda j: (0, jnp.maximum(j - count, 0)),
        ]
    specs = [pl.BlockSpec((shard, tile), index_map) for index_map in maps]
    return pl.pallas_call(
        settle_kernel,
        grid=(count * len(zero),),
        in_specs=[pl.BlockSpec(memory_space=pltpu.SMEM), *specs, *specs],
        out_specs=pl.BlockSpec((tile, shard), lambda j: (j, 0)),
        out_shape=jax.ShapeDtypeStruct((units, shard), F32),
        cost_estimate=pl.CostEstimate(
            flops=units * shard, bytes_accessed=8 * units * shard, transcendentals=0
        ),
        name="settle",
    )(flag, *zero, *one)


def step(layer_input, g_out, attn_gain, w_query, w_keyval, w_out, ffn_gain, w_gate, w_up, w_down):
    section = lax.axis_index("section")
    col = lax.axis_index("col")
    peer = lax.axis_index(ROW) % SPAN
    cols = lax.axis_size("col")
    is_first = section == 0
    is_key = col % 2 == 0
    rows = layer_input.shape[2]
    width = layer_input.shape[3]
    own_rows = rows // cols
    full = width * cols
    heads = w_query.shape[2] // HD
    query_cols = w_query.shape[2]
    qkv_cols = query_cols + HD
    units = w_gate.shape[2]
    scale = 1.0 / math.sqrt(HD)

    def by_section(first, second):
        return jnp.where(is_first, first, second)

    def by_key(first, second):
        return jnp.where(is_key, first, second)

    def xor_rows(block):
        return jnp.concatenate(
            [lax.dynamic_slice_in_dim(block, (col ^ k) * own_rows, own_rows, 0) for k in range(cols)],
            axis=0,
        )

    def reorder(block, k):
        parts = jnp.split(block, cols, axis=0)
        return jnp.concatenate([parts[m ^ k] for m in range(cols)], axis=0)

    def gather_width(block):
        parts = [reorder(part, k) for k, part in enumerate(gather_blocks(xor_rows(block)))]
        total = jnp.zeros((block.shape[0], full), block.dtype)
        for k, part in enumerate(parts):
            total = lax.dynamic_update_slice_in_dim(total, part, (col ^ k) * width, 1)
        return total

    def tokens_from_width(block):
        total = jnp.zeros((own_rows, full), block.dtype)
        for k in range(cols):
            part = lax.dynamic_slice_in_dim(block, (col ^ k) * own_rows, own_rows, 0)
            if k:
                part = over_col(part, k)
            total = lax.dynamic_update_slice_in_dim(total, part, (col ^ k) * width, 1)
        return total

    def width_from_tokens(block):
        total = jnp.zeros((rows, width), block.dtype)
        for k in range(cols):
            part = lax.dynamic_slice_in_dim(block, (col ^ k) * width, width, 1)
            if k:
                part = over_col(part, k)
            total = lax.dynamic_update_slice_in_dim(total, part, (col ^ k) * own_rows, 0)
        return total

    gains_own = jnp.stack([attn_gain[0], ffn_gain[0]])
    gains_other = over_section(gains_own)
    gains_part = jnp.stack([by_section(gains_own, gains_other), by_section(gains_other, gains_own)])
    gains = jnp.zeros((2, 2, full), F32)
    for k in range(cols):
        part = over_col(gains_part, k) if k else gains_part
        gains = lax.dynamic_update_slice_in_dim(gains, part, (col ^ k) * width, 2)

    shard = w_query.shape[1]
    attn_own = jnp.concatenate([w_query[0], w_keyval[0], w_out[0].T], axis=1)
    half_rows = shard // 2
    wide = -(-units // 256) * 256
    half_units = wide // 2

    def both_layers(low, high):
        got = over_section(by_section(high, low))
        return by_section(low, got), by_section(got, high)

    def widen(array):
        return jnp.pad(array, ((0, 0), (0, wide - units)))

    down_own = widen(w_down[0].T)
    attn_parts = both_layers(attn_own[:half_rows], attn_own[half_rows:])
    gate_up_parts = both_layers(widen(w_gate[0]), widen(w_up[0]))
    down_parts = both_layers(down_own[:, :half_units], down_own[:, half_units:])

    def gather_layers(part):
        return lax.all_gather(part, ("section", ROW), axis=0, tiled=True)

    def split_layers(both):
        return both[:full], both[full:]

    def split_attn(both, layer):
        first, out = layer * qkv_cols, 2 * qkv_cols + layer * query_cols
        return both[:, first : first + qkv_cols], both[:, out : out + query_cols]

    def gather_attn(part):
        return lax.all_gather(part, (ROW, "section"), axis=0, tiled=True)

    order = jnp.concatenate(
        [(col ^ k) * own_rows + jnp.arange(own_rows, dtype=jnp.int32) for k in range(cols)]
    )
    positions = peer * rows + order
    cosine, sine = rope_tables(positions, HD)
    signed = jnp.where(jnp.arange(HD) < HD // 2, -sine, sine)

    def swap_halves(values):
        return jnp.concatenate([values[:, HD // 2 :], values[:, : HD // 2]], axis=1)

    flags = jnp.stack([peer, jnp.where(is_key, 1, 0)]).astype(jnp.int32)
    own_cosine = by_key(cosine, jnp.ones_like(cosine))
    own_signed = by_key(signed, jnp.zeros_like(signed))
    tables = (cosine, signed, own_cosine, own_signed)

    def attn_forward(normed, attn_w):
        queries, own = project_turn(normed, *attn_w, tables, heads)
        first = over_col(own, 1)
        mine = [own] + [along_row(own, k) for k in range(1, SPAN)]
        later = over_col(jnp.concatenate(mine[1:], axis=0), 1)
        attended, lse, keys, values = attend(
            queries, mine, first, later, flags, order, heads, scale
        )
        return attended, (normed, queries, keys, values, lse, attended)

    def attn_out(resid, attended, attn_w):
        return resid + scatter_tokens(dot(attended, split_attn(*attn_w)[1], 1, 1).astype(BF))

    def ffn_gather(middle, ffn_gain):
        normed_own, inverse_ffn = norm(middle, ffn_gain)
        return gather_tokens(normed_own), inverse_ffn

    def ffn_in(normed_ffn, gate_up_w):
        gate_up_w = split_layers(gate_up_w)
        gate = dot(normed_ffn, gate_up_w[0], 1, 0)
        up = dot(normed_ffn, gate_up_w[1], 1, 0)
        return gate.astype(BF), up.astype(BF), (jax.nn.silu(gate) * up).astype(BF)

    def ffn_out(hidden, down_w):
        down_w = split_layers(down_w)
        out = dot(hidden[:, :half_units], down_w[0], 1, 1)
        return scatter_tokens((out + dot(hidden[:, half_units:], down_w[1], 1, 1)).astype(BF))

    def swap_add(left, first, second):
        got = over_section(dot(left, by_section(second, first), 0, 0).astype(BF))
        return (dot(left, by_section(first, second), 0, 0) + got.astype(F32)).astype(BF)

    def scatter_rows(total):
        return lax.psum_scatter(total, ROW, scatter_dimension=0, tiled=True)

    def down_grad(grad_branch, hidden):
        return swap_add(grad_branch, hidden[:, :half_units], hidden[:, half_units:])

    def ffn_backward(layer, grad_own, grad_branch, down_total, kept, ffn_gain, gate_up_w, down_w):
        middle, inverse_ffn, normed_ffn, gate, up = kept
        gate_up_w, down_w = split_layers(gate_up_w), split_layers(down_w)
        down_sum = scatter_rows(down_total)
        grad_hidden = jnp.concatenate(
            [dot(grad_branch, down_w[0], 1, 0), dot(grad_branch, down_w[1], 1, 0)], axis=1
        )
        gate, up = gate.astype(F32), up.astype(F32)
        sigma = jax.nn.sigmoid(gate)
        dgate = (grad_hidden * up * sigma * (1.0 + gate * (1.0 - sigma))).astype(BF)
        dup = (grad_hidden * gate * sigma).astype(BF)
        gate_up_total = swap_add(normed_ffn, dgate, dup)
        if layer == 0:
            dgate, dup, gate_up_total = after(dgate, dup, gate_up_total)
        grad_normed_ffn = (dot(dgate, gate_up_w[0], 1, 1) + dot(dup, gate_up_w[1], 1, 1)).astype(BF)
        grad_normed_ffn = scatter_tokens(grad_normed_ffn)
        if layer == 1:
            grad_normed_ffn, gate_up_total = after(grad_normed_ffn, gate_up_total)
        gate_up_sum = scatter_rows(gate_up_total)
        grad_middle, grad_gain_ffn = norm_backward(grad_normed_ffn, middle, inverse_ffn, ffn_gain)
        grad_middle = grad_own + grad_middle
        return grad_middle, gate_up_sum, down_sum, grad_gain_ffn

    def attn_backward(grad_middle, resid, inverse_attn, kept, attn_gain, attn_w, *others):
        normed, queries, keys, values, lse, attended = kept
        w_qkv, w_o = split_attn(*attn_w)
        grad_attn_out = gather_tokens(grad_middle.astype(BF))
        grad_attended = dot(grad_attn_out, w_o, 1, 0).astype(BF)
        grad_query_raw, grad_keep, grad_send = attend_back(
            queries, grad_attended, lse, keys, values, flags, order, cosine, signed, heads, scale
        )
        grad_keep = grad_keep + over_col(grad_send, 1).astype(F32)
        pieces = jnp.split(grad_keep, SPAN, axis=0)
        grad_mine = pieces[0]
        for k in range(1, SPAN):
            grad_mine = grad_mine + along_row(pieces[k].astype(BF), -k).astype(F32)
        grad_wout = dot(grad_attn_out, attended, 0, 0).astype(BF)
        grad_wquery = dot(normed, grad_query_raw, 0, 0).astype(BF)
        got = over_section(by_section(grad_wout, grad_wquery))
        early = by_section(grad_wquery, grad_wout).astype(F32) + got.astype(F32)
        grad_mine, early, *others = after(grad_mine, early.astype(BF), *others)
        grad_keyval = grad_mine * own_cosine - swap_halves(grad_mine) * own_signed
        grad_keyval = grad_keyval.astype(BF)
        late = dot(normed, grad_keyval, 0, 0).astype(BF)
        late = late.astype(F32) + over_section(late).astype(F32)
        total = jnp.concatenate([early, late.astype(BF)], axis=1)
        grad_normed = (
            dot(grad_query_raw, w_qkv[:, :query_cols], 1, 1)
            + dot(grad_keyval, w_qkv[:, query_cols:], 1, 1)
        ).astype(BF)
        grad_normed, total = after(scatter_tokens(grad_normed), total)
        attn_sum = scatter_rows(total)
        grad_resid, grad_gain_attn = norm_backward(grad_normed, resid, inverse_attn, attn_gain)
        grad_resid = grad_middle + grad_resid
        return grad_resid, attn_sum, grad_gain_attn, others

    def own_width(block):
        block = lax.dynamic_slice_in_dim(block, col * width, width, 1)
        return xor_rows(block)

    def core_swap(layer, block):
        return block, lax.ppermute(block, "section", [(1 - layer, layer)])

    def by_layer(first, second):
        first, first_got = first
        second, second_got = second
        return jnp.stack([by_section(first, second_got), by_section(first_got, second)])

    def to_core(layer, block):
        got = lax.ppermute(block, "section", [(1 - layer, layer)])
        return (block, got) if layer == 0 else (got, block)

    both = gather_attn(
        jnp.concatenate(
            [part[:, :qkv_cols] for part in attn_parts] + [part[:, qkv_cols:] for part in attn_parts],
            axis=1,
        )
    )
    attn_w = [(both, 0), (both, 1)]
    x_full = gather_width(lax.dynamic_index_in_dim(layer_input[:, 0], section, 0, keepdims=False))
    ffn_w = gather_layers(jnp.concatenate([gate_up_parts[0], down_parts[0]], axis=1))
    gate_up_w, down_w = [ffn_w[:, :wide]], [ffn_w[:, wide:]]
    normed, inverse = norm(x_full.astype(F32), gains[0, 0])
    resid_0, inverse_0 = x_full[:own_rows].astype(F32), inverse[:own_rows]
    attended, kept_attn_0 = attn_forward(normed, attn_w[0])
    middle = attn_out(resid_0, attended, attn_w[0])
    _, gate_up_part = after(middle, gate_up_parts[1])
    gate_up_w.append(gather_layers(gate_up_part))
    normed_ffn, inverse_ffn = ffn_gather(middle, gains[0, 1])
    gate, up, hidden = ffn_in(normed_ffn, gate_up_w[0])
    _, down_part = after(hidden, down_parts[1])
    down_w.append(gather_layers(down_part))
    result = middle + ffn_out(hidden, down_w[0])
    kept_ffn_0 = (middle, inverse_ffn, normed_ffn, gate, up)
    hidden_0 = hidden
    x_full = gather_tokens(result.astype(BF))
    act_0 = core_swap(0, own_width(x_full))
    normed, inverse = norm(x_full.astype(F32), gains[1, 0])
    resid_1, inverse_1 = x_full[:own_rows].astype(F32), inverse[:own_rows]
    attended, kept_attn_1 = attn_forward(normed, attn_w[1])
    _, g_out = after(attended, g_out)
    middle = attn_out(resid_1, attended, attn_w[1])
    normed_ffn, inverse_ffn = ffn_gather(middle, gains[1, 1])
    top = lax.dynamic_index_in_dim(g_out[:, 0], section, 0, keepdims=False)
    top_branch = gather_width(top.astype(BF))
    top_own = tokens_from_width(top)
    gate, up, hidden = ffn_in(normed_ffn, gate_up_w[1])
    down_w[1], down_total, top_own = after(down_w[1], down_grad(top_branch, hidden), top_own)
    result = middle + ffn_out(hidden, down_w[1])
    kept_ffn_1 = (middle, inverse_ffn, normed_ffn, gate, up)
    act_1 = core_swap(1, width_from_tokens(result.astype(BF)))
    acts = by_layer(act_0, act_1)

    grad_middle, gate_up_1, down_1, gain_ffn_1 = ffn_backward(
        1, top_own, top_branch, down_total, kept_ffn_1, gains[1, 1], gate_up_w[1], down_w[1]
    )
    grad_1, attn_1, gain_attn_1, (acts,) = attn_backward(
        grad_middle, resid_1, inverse_1, kept_attn_1, gains[1, 0], attn_w[1], acts
    )
    grad_1 = grad_1.astype(BF)
    branch = gather_tokens(grad_1)
    grads_1 = core_swap(1, own_width(branch))
    branch, down_total = after(branch, down_grad(branch, hidden_0))
    grad_middle, gate_up_0, down_0, gain_ffn_0 = ffn_backward(
        0, grad_1.astype(F32), branch, down_total, kept_ffn_0, gains[0, 1], gate_up_w[0], down_w[0]
    )
    grad_0, attn_0, gain_attn_0, _ = attn_backward(
        grad_middle, resid_0, inverse_0, kept_attn_0, gains[0, 0], attn_w[0]
    )
    grads_in = by_layer(core_swap(0, width_from_tokens(grad_0.astype(BF))), grads_1)

    def own_layer(first, second):
        return jax.tree.map(by_section, tuple(first), tuple(second))

    def final(zero, one):
        return own_layer(to_core(0, zero), to_core(1, one))

    flag = jnp.reshape(section, (1,)).astype(jnp.int32)
    gate_up_0, gate_up_1 = to_core(0, gate_up_0), to_core(1, gate_up_1)
    final_gate = settle(flag, gate_up_0[:1], gate_up_1[:1], units)
    final_up = settle(flag, gate_up_0[1:], gate_up_1[1:], units)
    final_down = settle(flag, to_core(0, down_0), to_core(1, down_1), units)
    attn_0, final_gate, final_up, final_down = after(attn_0, final_gate, final_up, final_down)
    final_query, final_out = final(attn_0[:, :query_cols], attn_1[:, :query_cols])
    final_keyval = by_section(attn_0[:, query_cols:], attn_1[:, query_cols:]).astype(F32)

    gain_grads_0 = jnp.stack([gain_attn_0, gain_ffn_0])
    gain_grads_1 = jnp.stack([gain_attn_1, gain_ffn_1])
    gain_sums = by_section(gain_grads_0, gain_grads_1) + over_section(
        by_section(gain_grads_1, gain_grads_0)
    )
    gain_parts = [
        lax.dynamic_slice_in_dim(gain_sums, (col ^ k) * width, width, 1) for k in range(cols)
    ]
    gain_sums = gain_parts[0] + sum(over_col(gain_parts[k], k) for k in range(1, cols))
    row_count = lax.axis_size(ROW)
    step = 1
    while step < row_count:
        gain_sums = gain_sums + lax.ppermute(
            gain_sums, ROW, [(i, i ^ step) for i in range(row_count)]
        )
        step *= 2

    return (
        acts.reshape(1, 2, 1, rows, width),
        grads_in.reshape(1, 2, 1, rows, width),
        gain_sums[:1],
        final_query[None].astype(F32),
        final_keyval[None],
        final_out.T[None].astype(F32),
        gain_sums[1:],
        final_gate.T[None],
        final_up.T[None],
        final_down[None],
    )


def solution(mesh):
    tokens = P(None, ROW, None, "col")
    gain = P("section", "col")
    rows_cols = P("section", ROW, "col")
    cols_rows = P("section", "col", ROW)
    layers = P("section", None, ROW, None, "col")
    return jax.shard_map(
        step,
        mesh=mesh,
        in_specs=(
            tokens,
            tokens,
            gain,
            rows_cols,
            rows_cols,
            cols_rows,
            gain,
            rows_cols,
            rows_cols,
            cols_rows,
        ),
        out_specs=(
            layers,
            layers,
            gain,
            rows_cols,
            rows_cols,
            cols_rows,
            gain,
            rows_cols,
            rows_cols,
            cols_rows,
        ),
        check_vma=False,
    )
```

```python
import functools
import math

import jax
import jax.numpy as jnp
from jax import lax
from jax.experimental import pallas as pl
from jax.experimental.pallas import tpu as pltpu
from jax.sharding import PartitionSpec as P


HD = 128
SPAN = 4
EPS = 1e-06
THETA = 1000000.0
BF = jnp.bfloat16
F32 = jnp.float32


def dot(left, right, left_dim, right_dim):
    return lax.dot_general(
        left, right, (((left_dim,), (right_dim,)), ((), ())), preferred_element_type=F32
    )


def rope_tables(positions, head_size):
    half = head_size // 2
    freqs = THETA ** (-(jnp.arange(half, dtype=F32) * 2.0) / head_size)
    angles = positions.astype(F32)[:, None] * freqs[None, :]
    angles = jnp.concatenate([angles, angles], axis=-1)
    return (jnp.cos(angles), jnp.sin(angles))


ROW = "row"


def after(value, *others):
    return lax.optimization_barrier((value, *others))


def over_col(block, step):
    count = lax.axis_size("col")
    return lax.ppermute(block, "col", [(i, i ^ step) for i in range(count)])


def over_section(block):
    return lax.ppermute(block, "section", [(0, 1), (1, 0)])


def along_row(block, steps):
    count = lax.axis_size(ROW)
    route = [(i, i + steps) for i in range(count) if 0 <= i % SPAN + steps < SPAN]
    return lax.ppermute(block, ROW, route)


def gather_blocks(own):
    half = own.shape[0] // 2
    first = over_col(own, 1)
    second = over_col(own, 2)
    third_low = over_col(first[:half], 2)
    third_high = over_col(second[half:], 1)
    return own, first, second, jnp.concatenate([third_low, third_high], axis=0)


def gather_tokens(own):
    return jnp.concatenate(gather_blocks(own), axis=0)


def scatter_tokens(partial):
    blocks = jnp.split(partial, 4, axis=0)
    got = [over_col(blocks[k], k).astype(F32) for k in (3, 1, 2)]
    return blocks[0].astype(F32) + got[0] + got[1] + got[2]


def norm(resid, gain):
    inverse = lax.rsqrt(jnp.mean(resid * resid, axis=1, keepdims=True) + EPS)
    return (resid * inverse * gain[None, :]).astype(BF), inverse


def norm_backward(grad_normed, resid, inverse, gain):
    scaled = resid * inverse
    grad_gain = jnp.sum(grad_normed * scaled, axis=0)
    grad_scaled = grad_normed * gain[None, :]
    mean_term = jnp.mean(grad_scaled * scaled, axis=1, keepdims=True)
    return inverse * (grad_scaled - scaled * mean_term), grad_gain


def qkv_kernel(heads, x_ref, w_ref, cos_ref, sign_ref, own_cos_ref, own_sign_ref, q_ref, own_ref):
    raw = jnp.dot(x_ref[...], w_ref[...], preferred_element_type=F32)
    for h in range(heads + 1):
        z = raw[:, h * HD : (h + 1) * HD]
        if h < heads:
            z = z * cos_ref[...] + pltpu.roll(z, HD // 2, 1) * sign_ref[...]
            q_ref[:, h * HD : (h + 1) * HD] = z.astype(BF)
        else:
            z = z * own_cos_ref[...] + pltpu.roll(z, HD // 2, 1) * own_sign_ref[...]
            own_ref[...] = z.astype(BF)


def project_turn(normed, weight, layer, tables, heads):
    rows, depth = normed.shape
    step = rows // 2
    cols = (heads + 1) * HD
    table = pl.BlockSpec((step, HD), lambda i: (i, 0))
    return pl.pallas_call(
        functools.partial(qkv_kernel, heads),
        grid=(2,),
        in_specs=[
            pl.BlockSpec((step, depth), lambda i: (i, 0)),
            pl.BlockSpec((depth, cols), lambda i: (0, layer)),
            *[table] * 4,
        ],
        out_specs=[
            pl.BlockSpec((step, heads * HD), lambda i: (i, 0)),
            pl.BlockSpec((step, HD), lambda i: (i, 0)),
        ],
        out_shape=[
            jax.ShapeDtypeStruct((rows, heads * HD), BF),
            jax.ShapeDtypeStruct((rows, HD), BF),
        ],
        cost_estimate=pl.CostEstimate(
            flops=2 * rows * depth * cols,
            bytes_accessed=2 * (rows * depth + depth * cols + rows * cols),
            transcendentals=0,
        ),
        name="project_turn",
    )(normed, weight, *tables)


def swapped(k, rows):
    quarter = rows // 4
    return [
        (pl.ds(k * rows + i * quarter, quarter), pl.ds((i ^ 1) * quarter, quarter)) for i in range(4)
    ]


def attend_kernel(scale, flag_ref, col_ref, row_ref, q_ref, *refs):
    mine, theirs = refs[:SPAN], refs[SPAN : 2 * SPAN]
    o_ref, lse_ref, k_ref, v_ref, e_ref, total_ref, acc_ref = refs[2 * SPAN :]
    rows = q_ref.shape[0]
    peer, is_key = flag_ref[0], flag_ref[1]
    q = q_ref[...]

    def place(own_ref, other_ref):
        for k in range(SPAN):
            own_ref[k * rows : (k + 1) * rows] = mine[k][...]
            for here, there in swapped(k, rows):
                other_ref[here] = theirs[k][there]

    @pl.when((pl.program_id(0) == 0) & (is_key == 1))
    def _():
        place(k_ref, v_ref)

    @pl.when((pl.program_id(0) == 0) & (is_key == 0))
    def _():
        place(v_ref, k_ref)

    def piece(ref, k):
        return ref[k * rows : (k + 1) * rows]

    def exps(k):
        s = lax.dot_general(
            piece(k_ref, k), q, (((1,), (1,)), ((), ())), preferred_element_type=F32
        )
        return jnp.exp(s * scale)

    e = jnp.where(col_ref[...] <= row_ref[...], exps(0), 0.0)
    e_ref[0] = e
    total_ref[...] = jnp.sum(e, axis=0, keepdims=True)
    for k in range(1, SPAN):

        @pl.when(peer >= k)
        def _():
            e = exps(k)
            e_ref[k] = e
            total_ref[...] += jnp.sum(e, axis=0, keepdims=True)

    total = total_ref[...]
    lse_ref[0] = jnp.log(total)
    shrink = jnp.where(total > 1.0, 2.0**-64, 1.0)
    inverse = 1.0 / (total * shrink)

    def term(k):
        p = ((e_ref[k] * shrink) * inverse).astype(BF)
        return lax.dot_general(
            piece(v_ref, k), p, (((0,), (0,)), ((), ())), preferred_element_type=F32
        )

    acc_ref[...] = term(0)
    for k in range(1, SPAN):

        @pl.when(peer >= k)
        def _():
            acc_ref[...] += term(k)

    o_ref[...] = acc_ref[...].T.astype(BF)


def attend(queries, mine, first, later, flags, order, heads, scale):
    rows = queries.shape[0]
    full = SPAN * rows
    piece = pl.BlockSpec((rows, HD), lambda h: (0, 0))
    whole = pl.BlockSpec((full, HD), lambda h: (0, 0))
    return pl.pallas_call(
        functools.partial(attend_kernel, scale),
        grid=(heads,),
        in_specs=[
            pl.BlockSpec(memory_space=pltpu.SMEM),
            pl.BlockSpec((rows, 1), lambda h: (0, 0)),
            pl.BlockSpec((1, rows), lambda h: (0, 0)),
            pl.BlockSpec((rows, HD), lambda h: (0, h)),
            *[piece] * SPAN,
            piece,
            *[pl.BlockSpec((rows, HD), lambda h, k=k: (k, 0)) for k in range(SPAN - 1)],
        ],
        out_specs=[
            pl.BlockSpec((rows, HD), lambda h: (0, h)),
            pl.BlockSpec((1, 1, rows), lambda h: (h, 0, 0)),
            whole,
            whole,
        ],
        out_shape=[
            jax.ShapeDtypeStruct((rows, heads * HD), BF),
            jax.ShapeDtypeStruct((heads, 1, rows), F32),
            jax.ShapeDtypeStruct((full, HD), BF),
            jax.ShapeDtypeStruct((full, HD), BF),
        ],
        scratch_shapes=[
            pltpu.VMEM((SPAN, rows, rows), F32),
            pltpu.VMEM((1, rows), F32),
            pltpu.VMEM((HD, rows), F32),
        ],
        cost_estimate=pl.CostEstimate(
            flops=4 * heads * rows * full * HD,
            bytes_accessed=4 * rows * HD * (heads + 2 * SPAN),
            transcendentals=heads * rows * full,
        ),
        name="attend",
    )(flags, order[:, None], order[None, :], queries, *mine, first, *[later] * (SPAN - 1))


def attend_back_kernel(
    scale, flag_ref, col_ref, row_ref, cos_ref, sign_ref, q_ref, do_ref, lse_ref, k_ref, v_ref,
    dq_ref, keep_ref, send_ref, p_ref, dp_ref, sum_ref, turn_ref, dk_ref, dv_ref,
):
    h = pl.program_id(0)
    last = pl.num_programs(0) - 1
    rows = q_ref.shape[0]
    peer, is_key = flag_ref[0], flag_ref[1]
    q, do = q_ref[...], do_ref[...]
    lse = lse_ref[0]

    def piece(ref, k):
        return ref[k * rows : (k + 1) * rows]

    def first(k):
        nt = (((1,), (1,)), ((), ()))
        s = lax.dot_general(piece(k_ref, k), q, nt, preferred_element_type=F32)
        p = jnp.exp(s * scale - lse)
        if k == 0:
            p = jnp.where(col_ref[...] <= row_ref[...], p, 0.0)
        dp = lax.dot_general(piece(v_ref, k), do, nt, preferred_element_type=F32)
        p_ref[k] = p
        dp_ref[k] = dp
        return jnp.sum(p * dp, axis=0, keepdims=True)

    def second(k):
        p = p_ref[k]
        ds = (p * (dp_ref[k] - sum_ref[...])).astype(BF)
        dk = jnp.dot(ds, q, preferred_element_type=F32)
        dv = jnp.dot(p.astype(BF), do, preferred_element_type=F32)

        @pl.when(h == 0)
        def _():
            dk_ref[k * rows : (k + 1) * rows] = dk
            dv_ref[k * rows : (k + 1) * rows] = dv

        @pl.when(h > 0)
        def _():
            dk_ref[k * rows : (k + 1) * rows] += dk
            dv_ref[k * rows : (k + 1) * rows] += dv

        return lax.dot_general(
            piece(k_ref, k), ds, (((0,), (0,)), ((), ())), preferred_element_type=F32
        )

    sum_ref[...] = first(0)
    for k in range(1, SPAN):

        @pl.when(peer >= k)
        def _():
            sum_ref[...] += first(k)

    turn_ref[...] = second(0)
    for k in range(1, SPAN):

        @pl.when(peer >= k)
        def _():
            turn_ref[...] += second(k)

        @pl.when((peer < k) & (h == 0))
        def _():
            dk_ref[k * rows : (k + 1) * rows] = jnp.zeros((rows, HD), F32)
            dv_ref[k * rows : (k + 1) * rows] = jnp.zeros((rows, HD), F32)

    dq = turn_ref[...].T * scale
    dq = dq * cos_ref[...] - pltpu.roll(dq, HD // 2, 1) * sign_ref[...]
    dq_ref[...] = dq.astype(BF)

    @pl.when((h == last) & (is_key == 1))
    def _():
        keep_ref[...] = dk_ref[...] * scale
        for k in range(SPAN):
            for here, there in swapped(k, rows):
                to = pl.ds(k * rows + there.start, there.size)
                send_ref[to] = dv_ref[here].astype(BF)

    @pl.when((h == last) & (is_key == 0))
    def _():
        keep_ref[...] = dv_ref[...]
        for k in range(SPAN):
            for here, there in swapped(k, rows):
                to = pl.ds(k * rows + there.start, there.size)
                send_ref[to] = (dk_ref[here] * scale).astype(BF)


def attend_back(queries, grads, lse, keys, values, flags, order, cosine, signed, heads, scale):
    rows = queries.shape[0]
    full = SPAN * rows
    whole = pl.BlockSpec((full, HD), lambda h: (0, 0))
    table = pl.BlockSpec((rows, HD), lambda h: (0, 0))
    one_head = pl.BlockSpec((rows, HD), lambda h: (0, h))
    return pl.pallas_call(
        functools.partial(attend_back_kernel, scale),
        grid=(heads,),
        in_specs=[
            pl.BlockSpec(memory_space=pltpu.SMEM),
            pl.BlockSpec((rows, 1), lambda h: (0, 0)),
            pl.BlockSpec((1, rows), lambda h: (0, 0)),
            table,
            table,
            one_head,
            one_head,
            pl.BlockSpec((1, 1, rows), lambda h: (h, 0, 0)),
            whole,
            whole,
        ],
        out_specs=[one_head, whole, whole],
        out_shape=[
            jax.ShapeDtypeStruct((rows, heads * HD), BF),
            jax.ShapeDtypeStruct((full, HD), F32),
            jax.ShapeDtypeStruct((full, HD), BF),
        ],
        scratch_shapes=[
            pltpu.VMEM((SPAN, rows, rows), F32),
            pltpu.VMEM((SPAN, rows, rows), F32),
            pltpu.VMEM((1, rows), F32),
            pltpu.VMEM((HD, rows), F32),
            pltpu.VMEM((full, HD), F32),
            pltpu.VMEM((full, HD), F32),
        ],
        cost_estimate=pl.CostEstimate(
            flops=10 * heads * rows * full * HD,
            bytes_accessed=4 * rows * HD * (2 * heads + 2 * SPAN),
            transcendentals=heads * rows * full,
        ),
        name="attend_back",
    )(flags, order[:, None], order[None, :], cosine, signed, queries, grads, lse, keys, values)


def settle_kernel(flag_ref, *refs):
    half, out_ref = len(refs) // 2, refs[-1]
    blocks = (refs[:half], refs[half:-1])
    for layer, parts in enumerate(blocks):
        for i, part in enumerate(parts):
            mine = flag_ref[0] == layer
            if len(parts) > 1:
                low = pl.program_id(0) < pl.num_programs(0) // 2
                mine = mine & (low if i == 0 else jnp.logical_not(low))

            @pl.when(mine)
            def _():
                out_ref[...] = part[...].astype(F32).T


def settle(flag, zero, one, units):
    shard = zero[0].shape[0]
    tile = zero[0].shape[1] // 3
    count = 3
    if len(zero) == 1:
        maps = [lambda j: (0, j)]
    else:
        maps = [
            lambda j: (0, jnp.minimum(j, count - 1)),
            lambda j: (0, jnp.maximum(j - count, 0)),
        ]
    specs = [pl.BlockSpec((shard, tile), index_map) for index_map in maps]
    return pl.pallas_call(
        settle_kernel,
        grid=(count * len(zero),),
        in_specs=[pl.BlockSpec(memory_space=pltpu.SMEM), *specs, *specs],
        out_specs=pl.BlockSpec((tile, shard), lambda j: (j, 0)),
        out_shape=jax.ShapeDtypeStruct((units, shard), F32),
        cost_estimate=pl.CostEstimate(
            flops=units * shard, bytes_accessed=8 * units * shard, transcendentals=0
        ),
        name="settle",
    )(flag, *zero, *one)


def step(layer_input, g_out, attn_gain, w_query, w_keyval, w_out, ffn_gain, w_gate, w_up, w_down):
    section = lax.axis_index("section")
    col = lax.axis_index("col")
    peer = lax.axis_index(ROW) % SPAN
    cols = lax.axis_size("col")
    is_first = section == 0
    is_key = col % 2 == 0
    rows = layer_input.shape[2]
    width = layer_input.shape[3]
    own_rows = rows // cols
    full = width * cols
    heads = w_query.shape[2] // HD
    query_cols = w_query.shape[2]
    qkv_cols = query_cols + HD
    units = w_gate.shape[2]
    scale = 1.0 / math.sqrt(HD)

    def by_section(first, second):
        return jnp.where(is_first, first, second)

    def by_key(first, second):
        return jnp.where(is_key, first, second)

    def xor_rows(block):
        return jnp.concatenate(
            [lax.dynamic_slice_in_dim(block, (col ^ k) * own_rows, own_rows, 0) for k in range(cols)],
            axis=0,
        )

    def reorder(block, k):
        parts = jnp.split(block, cols, axis=0)
        return jnp.concatenate([parts[m ^ k] for m in range(cols)], axis=0)

    def gather_width(block):
        parts = [reorder(part, k) for k, part in enumerate(gather_blocks(xor_rows(block)))]
        total = jnp.zeros((block.shape[0], full), block.dtype)
        for k, part in enumerate(parts):
            total = lax.dynamic_update_slice_in_dim(total, part, (col ^ k) * width, 1)
        return total

    def tokens_from_width(block):
        total = jnp.zeros((own_rows, full), block.dtype)
        for k in range(cols):
            part = lax.dynamic_slice_in_dim(block, (col ^ k) * own_rows, own_rows, 0)
            if k:
                part = over_col(part, k)
            total = lax.dynamic_update_slice_in_dim(total, part, (col ^ k) * width, 1)
        return total

    def width_from_tokens(block):
        total = jnp.zeros((rows, width), block.dtype)
        for k in range(cols):
            part = lax.dynamic_slice_in_dim(block, (col ^ k) * width, width, 1)
            if k:
                part = over_col(part, k)
            total = lax.dynamic_update_slice_in_dim(total, part, (col ^ k) * own_rows, 0)
        return total

    gains_own = jnp.stack([attn_gain[0], ffn_gain[0]])
    gains_other = over_section(gains_own)
    gains_part = jnp.stack([by_section(gains_own, gains_other), by_section(gains_other, gains_own)])
    gains = jnp.zeros((2, 2, full), F32)
    for k in range(cols):
        part = over_col(gains_part, k) if k else gains_part
        gains = lax.dynamic_update_slice_in_dim(gains, part, (col ^ k) * width, 2)

    shard = w_query.shape[1]
    attn_own = jnp.concatenate([w_query[0], w_keyval[0], w_out[0].T], axis=1)
    half_rows = shard // 2
    wide = -(-units // 256) * 256
    half_units = wide // 2

    def both_layers(low, high):
        got = over_section(by_section(high, low))
        return by_section(low, got), by_section(got, high)

    def widen(array):
        return jnp.pad(array, ((0, 0), (0, wide - units)))

    down_own = widen(w_down[0].T)
    attn_parts = both_layers(attn_own[:half_rows], attn_own[half_rows:])
    gate_up_parts = both_layers(widen(w_gate[0]), widen(w_up[0]))
    down_parts = both_layers(down_own[:, :half_units], down_own[:, half_units:])

    def gather_layers(part):
        return lax.all_gather(part, ("section", ROW), axis=0, tiled=True)

    def split_layers(both):
        return both[:full], both[full:]

    def split_attn(both, layer):
        first, out = layer * qkv_cols, 2 * qkv_cols + layer * query_cols
        return both[:, first : first + qkv_cols], both[:, out : out + query_cols]

    def gather_attn(part):
        return lax.all_gather(part, (ROW, "section"), axis=0, tiled=True)

    order = jnp.concatenate(
        [(col ^ k) * own_rows + jnp.arange(own_rows, dtype=jnp.int32) for k in range(cols)]
    )
    positions = peer * rows + order
    cosine, sine = rope_tables(positions, HD)
    signed = jnp.where(jnp.arange(HD) < HD // 2, -sine, sine)

    def swap_halves(values):
        return jnp.concatenate([values[:, HD // 2 :], values[:, : HD // 2]], axis=1)

    flags = jnp.stack([peer, jnp.where(is_key, 1, 0)]).astype(jnp.int32)
    own_cosine = by_key(cosine, jnp.ones_like(cosine))
    own_signed = by_key(signed, jnp.zeros_like(signed))
    tables = (cosine, signed, own_cosine, own_signed)

    def attn_forward(normed, attn_w):
        queries, own = project_turn(normed, *attn_w, tables, heads)
        first = over_col(own, 1)
        mine = [own] + [along_row(own, k) for k in range(1, SPAN)]
        later = over_col(jnp.concatenate(mine[1:], axis=0), 1)
        attended, lse, keys, values = attend(
            queries, mine, first, later, flags, order, heads, scale
        )
        return attended, (normed, queries, keys, values, lse, attended)

    def attn_out(resid, attended, attn_w):
        return resid + scatter_tokens(dot(attended, split_attn(*attn_w)[1], 1, 1).astype(BF))

    def ffn_gather(middle, ffn_gain):
        normed_own, inverse_ffn = norm(middle, ffn_gain)
        return gather_tokens(normed_own), inverse_ffn

    def ffn_in(normed_ffn, gate_up_w):
        gate_up_w = split_layers(gate_up_w)
        gate = dot(normed_ffn, gate_up_w[0], 1, 0)
        up = dot(normed_ffn, gate_up_w[1], 1, 0)
        return gate.astype(BF), up.astype(BF), (jax.nn.silu(gate) * up).astype(BF)

    def ffn_out(hidden, down_w):
        down_w = split_layers(down_w)
        out = dot(hidden[:, :half_units], down_w[0], 1, 1)
        return scatter_tokens((out + dot(hidden[:, half_units:], down_w[1], 1, 1)).astype(BF))

    def swap_add(left, first, second):
        got = over_section(dot(left, by_section(second, first), 0, 0).astype(BF))
        return (dot(left, by_section(first, second), 0, 0) + got.astype(F32)).astype(BF)

    def scatter_rows(total):
        return lax.psum_scatter(total, ROW, scatter_dimension=0, tiled=True)

    def down_grad(grad_branch, hidden):
        return swap_add(grad_branch, hidden[:, :half_units], hidden[:, half_units:])

    def ffn_backward(layer, grad_own, grad_branch, down_total, kept, ffn_gain, gate_up_w, down_w):
        middle, inverse_ffn, normed_ffn, gate, up = kept
        gate_up_w, down_w = split_layers(gate_up_w), split_layers(down_w)
        down_sum = scatter_rows(down_total)
        grad_hidden = jnp.concatenate(
            [dot(grad_branch, down_w[0], 1, 0), dot(grad_branch, down_w[1], 1, 0)], axis=1
        )
        gate, up = gate.astype(F32), up.astype(F32)
        sigma = jax.nn.sigmoid(gate)
        dgate = (grad_hidden * up * sigma * (1.0 + gate * (1.0 - sigma))).astype(BF)
        dup = (grad_hidden * gate * sigma).astype(BF)
        gate_up_total = swap_add(normed_ffn, dgate, dup)
        if layer == 0:
            dgate, dup, gate_up_total = after(dgate, dup, gate_up_total)
        grad_normed_ffn = (dot(dgate, gate_up_w[0], 1, 1) + dot(dup, gate_up_w[1], 1, 1)).astype(BF)
        grad_normed_ffn = scatter_tokens(grad_normed_ffn)
        if layer == 1:
            grad_normed_ffn, gate_up_total = after(grad_normed_ffn, gate_up_total)
        gate_up_sum = scatter_rows(gate_up_total)
        grad_middle, grad_gain_ffn = norm_backward(grad_normed_ffn, middle, inverse_ffn, ffn_gain)
        grad_middle = grad_own + grad_middle
        return grad_middle, gate_up_sum, down_sum, grad_gain_ffn

    def attn_backward(grad_middle, resid, inverse_attn, kept, attn_gain, attn_w, *others):
        normed, queries, keys, values, lse, attended = kept
        w_qkv, w_o = split_attn(*attn_w)
        grad_attn_out = gather_tokens(grad_middle.astype(BF))
        grad_attended = dot(grad_attn_out, w_o, 1, 0).astype(BF)
        grad_query_raw, grad_keep, grad_send = attend_back(
            queries, grad_attended, lse, keys, values, flags, order, cosine, signed, heads, scale
        )
        grad_keep = grad_keep + over_col(grad_send, 1).astype(F32)
        pieces = jnp.split(grad_keep, SPAN, axis=0)
        grad_mine = pieces[0]
        for k in range(1, SPAN):
            grad_mine = grad_mine + along_row(pieces[k].astype(BF), -k).astype(F32)
        grad_wout = dot(grad_attn_out, attended, 0, 0).astype(BF)
        grad_wquery = dot(normed, grad_query_raw, 0, 0).astype(BF)
        got = over_section(by_section(grad_wout, grad_wquery))
        early = by_section(grad_wquery, grad_wout).astype(F32) + got.astype(F32)
        grad_mine, early, *others = after(grad_mine, early.astype(BF), *others)
        grad_keyval = grad_mine * own_cosine - swap_halves(grad_mine) * own_signed
        grad_keyval = grad_keyval.astype(BF)
        late = dot(normed, grad_keyval, 0, 0).astype(BF)
        late = late.astype(F32) + over_section(late).astype(F32)
        total = jnp.concatenate([early, late.astype(BF)], axis=1)
        grad_normed = (
            dot(grad_query_raw, w_qkv[:, :query_cols], 1, 1)
            + dot(grad_keyval, w_qkv[:, query_cols:], 1, 1)
        ).astype(BF)
        grad_normed, total = after(scatter_tokens(grad_normed), total)
        attn_sum = scatter_rows(total)
        grad_resid, grad_gain_attn = norm_backward(grad_normed, resid, inverse_attn, attn_gain)
        grad_resid = grad_middle + grad_resid
        return grad_resid, attn_sum, grad_gain_attn, others

    def own_width(block):
        block = lax.dynamic_slice_in_dim(block, col * width, width, 1)
        return xor_rows(block)

    def core_swap(layer, block):
        return block, lax.ppermute(block, "section", [(1 - layer, layer)])

    def by_layer(first, second):
        first, first_got = first
        second, second_got = second
        return jnp.stack([by_section(first, second_got), by_section(first_got, second)])

    def to_core(layer, block):
        got = lax.ppermute(block, "section", [(1 - layer, layer)])
        return (block, got) if layer == 0 else (got, block)

    both = gather_attn(
        jnp.concatenate(
            [part[:, :qkv_cols] for part in attn_parts] + [part[:, qkv_cols:] for part in attn_parts],
            axis=1,
        )
    )
    attn_w = [(both, 0), (both, 1)]
    x_full = gather_width(lax.dynamic_index_in_dim(layer_input[:, 0], section, 0, keepdims=False))
    ffn_w = gather_layers(jnp.concatenate([gate_up_parts[0], down_parts[0]], axis=1))
    gate_up_w, down_w = [ffn_w[:, :wide]], [ffn_w[:, wide:]]
    normed, inverse = norm(x_full.astype(F32), gains[0, 0])
    resid_0, inverse_0 = x_full[:own_rows].astype(F32), inverse[:own_rows]
    attended, kept_attn_0 = attn_forward(normed, attn_w[0])
    middle = attn_out(resid_0, attended, attn_w[0])
    _, gate_up_part = after(middle, gate_up_parts[1])
    gate_up_w.append(gather_layers(gate_up_part))
    normed_ffn, inverse_ffn = ffn_gather(middle, gains[0, 1])
    gate, up, hidden = ffn_in(normed_ffn, gate_up_w[0])
    _, down_part = after(hidden, down_parts[1])
    down_w.append(gather_layers(down_part))
    result = middle + ffn_out(hidden, down_w[0])
    kept_ffn_0 = (middle, inverse_ffn, normed_ffn, gate, up)
    hidden_0 = hidden
    x_full = gather_tokens(result.astype(BF))
    act_0 = core_swap(0, own_width(x_full))
    normed, inverse = norm(x_full.astype(F32), gains[1, 0])
    resid_1, inverse_1 = x_full[:own_rows].astype(F32), inverse[:own_rows]
    attended, kept_attn_1 = attn_forward(normed, attn_w[1])
    _, g_out = after(attended, g_out)
    middle = attn_out(resid_1, attended, attn_w[1])
    normed_ffn, inverse_ffn = ffn_gather(middle, gains[1, 1])
    top = lax.dynamic_index_in_dim(g_out[:, 0], section, 0, keepdims=False)
    top_branch = gather_width(top.astype(BF))
    top_own = tokens_from_width(top)
    gate, up, hidden = ffn_in(normed_ffn, gate_up_w[1])
    down_w[1], down_total, top_own = after(down_w[1], down_grad(top_branch, hidden), top_own)
    result = middle + ffn_out(hidden, down_w[1])
    kept_ffn_1 = (middle, inverse_ffn, normed_ffn, gate, up)
    act_1 = core_swap(1, width_from_tokens(result.astype(BF)))
    acts = by_layer(act_0, act_1)

    grad_middle, gate_up_1, down_1, gain_ffn_1 = ffn_backward(
        1, top_own, top_branch, down_total, kept_ffn_1, gains[1, 1], gate_up_w[1], down_w[1]
    )
    grad_1, attn_1, gain_attn_1, (acts,) = attn_backward(
        grad_middle, resid_1, inverse_1, kept_attn_1, gains[1, 0], attn_w[1], acts
    )
    grad_1 = grad_1.astype(BF)
    branch = gather_tokens(grad_1)
    grads_1 = core_swap(1, own_width(branch))
    branch, down_total = after(branch, down_grad(branch, hidden_0))
    grad_middle, gate_up_0, down_0, gain_ffn_0 = ffn_backward(
        0, grad_1.astype(F32), branch, down_total, kept_ffn_0, gains[0, 1], gate_up_w[0], down_w[0]
    )
    flag = jnp.reshape(section, (1,)).astype(jnp.int32)
    grad_0, attn_0, gain_attn_0, others = attn_backward(
        grad_middle, resid_0, inverse_0, kept_attn_0, gains[0, 0], attn_w[0],
        settle(flag, to_core(0, down_0), to_core(1, down_1), units),
        *to_core(1, gate_up_1),
        *to_core(1, attn_1[:, :query_cols]),
        *grads_1,
    )
    final_down, gate_up_1, attn_1_out, grads_1 = others[0], others[1:3], others[3:5], others[5:]
    grads_in = by_layer(core_swap(0, width_from_tokens(grad_0.astype(BF))), grads_1)

    def own_layer(first, second):
        return jax.tree.map(by_section, tuple(first), tuple(second))

    gate_up_0 = to_core(0, gate_up_0)
    final_gate = settle(flag, gate_up_0[:1], gate_up_1[:1], units)
    final_up = settle(flag, gate_up_0[1:], gate_up_1[1:], units)
    attn_0, final_gate, final_up = after(attn_0, final_gate, final_up)
    final_query, final_out = own_layer(to_core(0, attn_0[:, :query_cols]), attn_1_out)
    final_keyval = by_section(attn_0[:, query_cols:], attn_1[:, query_cols:]).astype(F32)

    gain_grads_0 = jnp.stack([gain_attn_0, gain_ffn_0])
    gain_grads_1 = jnp.stack([gain_attn_1, gain_ffn_1])
    gain_sums = by_section(gain_grads_0, gain_grads_1) + over_section(
        by_section(gain_grads_1, gain_grads_0)
    )
    gain_parts = [
        lax.dynamic_slice_in_dim(gain_sums, (col ^ k) * width, width, 1) for k in range(cols)
    ]
    gain_sums = gain_parts[0] + sum(over_col(gain_parts[k], k) for k in range(1, cols))
    row_count = lax.axis_size(ROW)
    step = 1
    while step < row_count:
        gain_sums = gain_sums + lax.ppermute(
            gain_sums, ROW, [(i, i ^ step) for i in range(row_count)]
        )
        step *= 2

    return (
        acts.reshape(1, 2, 1, rows, width),
        grads_in.reshape(1, 2, 1, rows, width),
        gain_sums[:1],
        final_query[None].astype(F32),
        final_keyval[None],
        final_out.T[None].astype(F32),
        gain_sums[1:],
        final_gate.T[None],
        final_up.T[None],
        final_down[None],
    )


def solution(mesh):
    tokens = P(None, ROW, None, "col")
    gain = P("section", "col")
    rows_cols = P("section", ROW, "col")
    cols_rows = P("section", "col", ROW)
    layers = P("section", None, ROW, None, "col")
    return jax.shard_map(
        step,
        mesh=mesh,
        in_specs=(
            tokens,
            tokens,
            gain,
            rows_cols,
            rows_cols,
            cols_rows,
            gain,
            rows_cols,
            rows_cols,
            cols_rows,
        ),
        out_specs=(
            layers,
            layers,
            gain,
            rows_cols,
            rows_cols,
            cols_rows,
            gain,
            rows_cols,
            rows_cols,
            cols_rows,
        ),
        check_vma=False,
    )
```
